256 devices in a mesh: dp: 4 (over x), expert: 64 (over z, y, core).
Axes of the slice: x: 4, y: 4, z: 8, core: 2. Of those that a mesh axis runs over, the one named last changes fastest.
Arguments:
- cell_table: bfloat16 [524288, 256], P(('dp', 'expert')), may hold values from -6 to 6
- sample_index: int32 [262144], P(('dp', 'expert')), may hold values from 0 to 2047
- region: int32 [262144, 1], P(('dp', 'expert')), may hold values from 0 to 63; in each aligned block of 1024 rows (0 to 1023, 1024 to 2047, ...) at most 32 rows name the same one
- targets: bfloat16 [262144, 256], P(('dp', 'expert')), may hold values from -6 to 6
- trunk_weight: bfloat16 [256, 256], replicated, may hold values from -0.375 to 0.375
- expert_params: float32 [64, 2, 256, 2048], P('expert', None, None, 'dp'), may hold values from -0.375 to 0.375
- first_moment: float32 [64, 2, 256, 2048], P('expert', None, None, 'dp'), may hold values from -4 to 4
- second_moment: float32 [64, 2, 256, 2048], P('expert', None, None, 'dp'), may hold values from 0.05 to 1
Outputs:
- trunk_grad: float32 [256, 256], replicated
- row_loss: float32 [262144], P(('dp', 'expert'))
- new_params: float32 [64, 2, 256, 2048], P('expert', None, None, 'dp')
- new_first: float32 [64, 2, 256, 2048], P('expert', None, None, 'dp')
- new_second: float32 [64, 2, 256, 2048], P('expert', None, None, 'dp')
The draws below stay inside these ranges and needn't reach their ends.
Inputs may be any that keep to these rules, and one draw needn't show every extreme that they name: In the 1024 rows of one device no region is named more than 32 times; some region exactly 32 times. `sample_index`: indexes the rows of the same device's block of cell_table.
All inputs are finite; a program needn't handle non-finite values.
Results may differ from the reference program's by a relative error of at most 0.0044.
Values may be sent and summed in bfloat16 or wider, within the bound.
A program may use at most 128 MiB of HBM per device.

```python
import math
import jax
import jax.numpy as jnp
import numpy as np
from jax import lax

D = 256
HID = 2048
ROWS_DEV = 1024
CELLS_DEV = 2048
EXPERTS = 64
CAP = 32
TOKENS = 262144
CELLS = 524288
N_DP = 4
N_EXPERT = 64


def with_ends(result, key, low, largest):
    dims = result.shape
    spot = [jax.random.randint(jax.random.fold_in(key, axis), (), 0, dims[axis]) for axis in range(len(dims))]
    result = result.at[tuple(spot)].set(low)
    longest = dims.index(max(dims))
    spot[longest] = (spot[longest] + 1) % dims[longest]
    return result.at[tuple(spot)].set(largest)


def level_of(stream_key, extent, shards, low, top_value):
    loudness, own = 1.0, jax.random.fold_in(stream_key, 6)
    for position, blocks in shards:
        steps = jnp.exp(jax.random.uniform(jax.random.fold_in(own, position), (blocks,), jnp.float32, low / len(shards), top_value / len(shards)))
        loudness = loudness * jnp.repeat(steps, extent[position] // blocks).reshape([-1 if axis == position else 1 for axis in range(len(extent))])
    return loudness


def assign_block(stream_key, own, number, rows, count, top, bound, lean):
    order = jax.random.permutation(stream_key, count)
    heavy_load, usual = shares(count, rows * top, bound, lean, True), shares(count, rows * top, bound, lean, False)
    places = jnp.arange(count)

    def named(lengths, offset_by):
        used = int((lengths > 0).sum())
        fixed = max(1, used // 4)
        shifted = fixed + (places - fixed + offset_by * (used - fixed)) % max(1, count - fixed)
        return jnp.zeros((count,), jnp.int32).at[order[jnp.where(places < fixed, places, shifted)]].set(jnp.asarray(lengths, jnp.int32))

    lengths = jnp.where(number % 4 == 0, named(heavy_load, number // 4), named(usual, number - number // 4 - 1))
    mixed = jax.random.permutation(jax.random.fold_in(own, 3), count)
    source_of, sink = mixed[0:count // 2 * 2:2], mixed[1:count // 2 * 2:2]
    margin = jnp.minimum(lengths[source_of] - 1, bound - lengths[sink]) // 2
    margin = jnp.where((source_of == order[0]) | (sink == order[0]) | (lengths[sink] == 0), 0, jnp.maximum(margin, 0))
    shifted = jax.random.randint(jax.random.fold_in(own, 4), (count // 2,), 0, 1 << 20) % (margin + 1)
    lengths = lengths.at[source_of].add(-shifted).at[sink].add(shifted)
    labels = jnp.searchsorted(jnp.cumsum(lengths), jnp.arange(rows * top), side="right").astype(jnp.int32)
    grid = labels.reshape(top, rows).T
    grid = grid[jax.random.permutation(jax.random.fold_in(own, 1), rows)]
    offset_by = jax.random.randint(jax.random.fold_in(own, 2), (rows, 1), 0, top)
    return jnp.take_along_axis(grid, (jnp.arange(top)[None, :] + offset_by) % top, axis=1)


def shares(amount, total, most, slope, full):
    portions = [(1 << 20) // math.isqrt(standing ** slope) + 1 for standing in range(1, amount + 1)]
    largest = most if full else min(most, max(-(-total // amount), total * portions[0] // sum(portions)))
    least = 1 if total - largest >= amount - 1 else 0
    given, rest = [largest] + [least] * (amount - 1), total - largest - least * (amount - 1)
    while rest > 0:
        movable = [i for i in range(1, amount) if given[i] < largest] or [i for i in range(1, amount) if given[i] < most]
        whole, budget = sum([portions[i] for i in movable]), rest
        for i in movable:
            more = min(most - given[i], max(1, budget * portions[i] // whole), rest)
            given[i] = given[i] + more
            rest = rest - more
    return np.array(given)


def centred(key, shape, width, bound, pieces=(), held_as=jnp.bfloat16):
    gain = level_of(key, shape, pieces, -0.22, 0.18) if pieces else 1.0
    entries = jax.random.normal(key, shape, jnp.float32) * width * gain
    return jnp.minimum(jnp.maximum(entries, -bound), bound).astype(held_as)


def setup_inputs(seed: int = 0) -> dict:
    arg_keys = jax.random.split(jax.random.key(seed), 9)
    cell_table = centred(arg_keys[0], (CELLS, D), 1.0, 6.0, ((0, 256),))
    sample_index = with_ends(jax.random.randint(arg_keys[1], (TOKENS,), 0, CELLS_DEV), jax.random.fold_in(arg_keys[1], 1), 0, CELLS_DEV - 1).astype(jnp.int32)
    region_keys = jax.random.split(jax.random.fold_in(arg_keys[2], 1), TOKENS // ROWS_DEV)
    region_turns = jax.random.permutation(jax.random.fold_in(arg_keys[2], 3), TOKENS // ROWS_DEV)
    region = jax.vmap(lambda own, number: assign_block(jax.random.fold_in(arg_keys[2], 2), own, number, ROWS_DEV, EXPERTS, 1, CAP, 2))(region_keys, region_turns).reshape((TOKENS, 1))
    targets = centred(arg_keys[3], (TOKENS, D), 1.0, 6.0, ((0, 256),))
    trunk_weight = centred(arg_keys[4], (D, D), D ** -0.5, 0.375)
    expert_params = centred(arg_keys[5], (EXPERTS, 2, D, HID), D ** -0.5, 0.375, ((0, 64), (3, 4)), jnp.float32)
    first_moment = centred(arg_keys[6], (EXPERTS, 2, D, HID), 0.3, 4.0, ((0, 64), (3, 4)), jnp.float32)
    second_moment = jnp.clip(jnp.exp(math.log(1.0) - 2.9957323 * jax.random.uniform(arg_keys[7], (EXPERTS, 2, D, HID), jnp.float32) ** level_of(arg_keys[7], (EXPERTS, 2, D, HID), ((0, 64), (3, 4)), -0.2, 0.2)), 0.05, 1.0)
    return {"cell_table": cell_table, "sample_index": sample_index, "region": region, "targets": targets, "trunk_weight": trunk_weight, "expert_params": expert_params, "first_moment": first_moment, "second_moment": second_moment}


loss_scale = 1.0 / 32.0
beta_one = 0.9
beta_two = 0.999
learn_rate = 0.05
adam_eps = 1e-08
adam_step = 10

def silu_slope(values):
    sigma = jax.nn.sigmoid(values)
    return sigma * (1.0 + values * (1.0 - sigma))

def expert_forward(arrived, w_up, w_down):
    up_pre = jnp.dot(arrived, w_up, preferred_element_type=jnp.float32)
    hidden = jax.nn.silu(up_pre).astype(jnp.bfloat16)
    predicted = lax.dot_general(hidden, w_down, (((1,), (1,)), ((), ())), preferred_element_type=jnp.float32)
    return (up_pre, hidden, predicted)

def expert_backward(arrived, up_pre, hidden, scaled_error, w_up, w_down):
    grad_down = lax.dot_general(scaled_error, hidden, (((0,), (0,)), ((), ())), preferred_element_type=jnp.float32)
    hidden_grad = jnp.dot(scaled_error, w_down, preferred_element_type=jnp.float32)
    pre_grad = (hidden_grad * silu_slope(up_pre)).astype(jnp.bfloat16)
    grad_up = lax.dot_general(arrived, pre_grad, (((0,), (0,)), ((), ())), preferred_element_type=jnp.float32)
    input_grad = lax.dot_general(pre_grad, w_up, (((1,), (1,)), ((), ())), preferred_element_type=jnp.float32).astype(jnp.bfloat16)
    return (grad_up, grad_down, input_grad)

def error_terms(predicted, target):
    errors = predicted - target.astype(jnp.float32)
    losses = lax.optimization_barrier(jnp.sum(errors * errors, axis=1)) * (0.5 * loss_scale)
    return (losses, (errors * loss_scale).astype(jnp.bfloat16))

def adam_update(params, first, second, grads):
    first_new = beta_one * first + (1.0 - beta_one) * grads
    second_new = beta_two * second + (1.0 - beta_two) * grads * grads
    first_hat = first_new / (1.0 - beta_one ** adam_step)
    second_hat = second_new / (1.0 - beta_two ** adam_step)
    return (params - learn_rate * first_hat / (jnp.sqrt(second_hat) + adam_eps), first_new, second_new)

def reference(cell_table, sample_index, region, targets, trunk_weight, expert_params, first_moment, second_moment):
    devices_all = N_DP * N_EXPERT
    experts = N_EXPERT
    table = cell_table.reshape(devices_all, CELLS_DEV, D)
    picks = sample_index.reshape(devices_all, ROWS_DEV)
    features = jax.vmap(lambda shard_rows, picked: jnp.take(shard_rows, picked, axis=0))(table, picks).reshape(-1, D)
    trunk_pre = jnp.dot(features, trunk_weight, preferred_element_type=jnp.float32)
    trunk_out = (features.astype(jnp.float32) + jax.nn.silu(trunk_pre)).astype(jnp.bfloat16)
    routed = region[:, 0].reshape(devices_all, ROWS_DEV)
    onehot = (routed[:, :, None] == jnp.arange(experts, dtype=jnp.int32)[None, None, :]).astype(jnp.int32)
    slots = lax.optimization_barrier(jnp.sum(jnp.cumsum(onehot, axis=1) * onehot, axis=2)) - 1
    device_ids = jnp.arange(devices_all, dtype=jnp.int32)[:, None]
    group_ids = device_ids // N_EXPERT
    source_ids = device_ids % N_EXPERT
    places = (((routed * N_DP + group_ids) * N_EXPERT + source_ids) * CAP + slots).reshape(-1).astype(jnp.int32)
    total = experts * N_DP * N_EXPERT * CAP
    inputs_buffer = jnp.zeros((total, D), jnp.bfloat16).at[places].set(trunk_out).reshape(experts, N_DP, N_EXPERT * CAP, D)
    target_buffer = jnp.zeros((total, D), jnp.bfloat16).at[places].set(targets).reshape(experts, N_DP, N_EXPERT * CAP, D)
    weights = expert_params.astype(jnp.bfloat16)

    def per_expert(operands):
        arrived_all, target_all, weight_pair = operands
        grad_up = jnp.zeros((D, HID), jnp.float32)
        grad_down = jnp.zeros((D, HID), jnp.float32)
        losses = []
        inputs_grads = []
        for group in range(N_DP):
            up_pre, hidden, predicted = expert_forward(arrived_all[group], weight_pair[0], weight_pair[1])
            slot_loss, scaled_error = error_terms(predicted, target_all[group])
            part_up, part_down, input_grad = expert_backward(arrived_all[group], up_pre, hidden, scaled_error, weight_pair[0], weight_pair[1])
            grad_up = grad_up + part_up
            grad_down = grad_down + part_down
            losses.append(slot_loss)
            inputs_grads.append(input_grad)
        return (jnp.stack(losses), jnp.stack(inputs_grads), jnp.stack([grad_up, grad_down]))
    slot_losses, input_grads, grads = lax.map(per_expert, (inputs_buffer, target_buffer, weights))
    row_grad = input_grads.reshape(-1, D)[places]
    row_loss = slot_losses.reshape(-1)[places]
    trunk_slope = (row_grad.astype(jnp.float32) * silu_slope(trunk_pre)).astype(jnp.bfloat16)
    trunk_grad = lax.dot_general(features, trunk_slope, (((0,), (0,)), ((), ())), preferred_element_type=jnp.float32)
    new_params, new_first, new_second = adam_update(expert_params, first_moment, second_moment, grads)
    return (trunk_grad, row_loss, new_params, new_first, new_second)
```

```python
import jax
import jax.numpy as jnp
from jax import lax
from jax.sharding import PartitionSpec as P

loss_scale = 1.0 / 32.0
beta_one = 0.9
beta_two = 0.999
learn_rate = 0.05
adam_eps = 1e-08
adam_step = 10


def silu_slope(values):
    sigma = jax.nn.sigmoid(values)
    return sigma * (1.0 + values * (1.0 - sigma))


def adam_update(params, first, second, grads):
    first_new = beta_one * first + (1.0 - beta_one) * grads
    second_new = beta_two * second + (1.0 - beta_two) * grads * grads
    first_hat = first_new / (1.0 - beta_one**adam_step)
    second_hat = second_new / (1.0 - beta_two**adam_step)
    return (
        params - learn_rate * first_hat / (jnp.sqrt(second_hat) + adam_eps),
        first_new,
        second_new,
    )


def on_device(
    cell_table,
    sample_index,
    region,
    targets,
    trunk_weight,
    expert_params,
    first_moment,
    second_moment,
):
    rows = sample_index.shape[0]
    width = cell_table.shape[1]
    experts = lax.axis_size("expert")
    capacity = 2 * rows // experts
    features = jnp.take(cell_table, sample_index, axis=0)
    routed = region[:, 0]
    onehot = (routed[:, None] == jnp.arange(experts, dtype=jnp.int32)[None, :]).astype(jnp.int32)
    slots = jnp.sum(jnp.cumsum(onehot, axis=0) * onehot, axis=1) - 1
    places = routed * capacity + slots

    gathered = lax.all_gather(expert_params.astype(jnp.bfloat16), "dp", axis=3, tiled=True)
    w_up = gathered[0, 0]
    w_down = gathered[0, 1]

    payload = jnp.concatenate([features, targets], axis=1)
    packed = jnp.zeros((experts * capacity, 2 * width), jnp.bfloat16).at[places].set(payload)
    arrived = lax.all_to_all(
        packed.reshape(experts, capacity, 2 * width), "expert", split_axis=0, concat_axis=0, tiled=True
    ).reshape(-1, 2 * width)
    feats = arrived[:, :width]
    there = arrived[:, width:]

    trunk_pre = jnp.dot(feats, trunk_weight, preferred_element_type=jnp.float32)
    trunk_out = (feats.astype(jnp.float32) + jax.nn.silu(trunk_pre)).astype(jnp.bfloat16)
    up_pre = jnp.dot(trunk_out, w_up, preferred_element_type=jnp.float32)
    hidden = jax.nn.silu(up_pre).astype(jnp.bfloat16)
    predicted = lax.dot_general(
        hidden, w_down, (((1,), (1,)), ((), ())), preferred_element_type=jnp.float32
    )
    errors = predicted - there.astype(jnp.float32)
    losses = jnp.sum(errors * errors, axis=1) * (0.5 * loss_scale)
    scaled = (errors * loss_scale).astype(jnp.bfloat16)
    back = lax.all_to_all(
        losses.reshape(experts, capacity), "expert", split_axis=0, concat_axis=0, tiled=True
    )
    row_loss = back.reshape(-1)[places]
    grad_down = lax.dot_general(
        scaled, hidden, (((0,), (0,)), ((), ())), preferred_element_type=jnp.float32
    )
    hidden_grad = jnp.dot(scaled, w_down, preferred_element_type=jnp.float32)
    pre_grad = (hidden_grad * silu_slope(up_pre)).astype(jnp.bfloat16)
    grad_up = lax.dot_general(
        trunk_out, pre_grad, (((0,), (0,)), ((), ())), preferred_element_type=jnp.float32
    )
    row_grad = lax.dot_general(
        pre_grad, w_up, (((1,), (1,)), ((), ())), preferred_element_type=jnp.float32
    ).astype(jnp.bfloat16)
    trunk_slope = (row_grad.astype(jnp.float32) * silu_slope(trunk_pre)).astype(jnp.bfloat16)
    trunk_local = lax.dot_general(
        feats, trunk_slope, (((0,), (0,)), ((), ())), preferred_element_type=jnp.float32
    )
    trunk_grad = lax.psum(trunk_local, ("dp", "expert"))
    grads = jnp.stack([grad_up, grad_down])[None]
    grad_shard = lax.psum_scatter(grads, "dp", scatter_dimension=3, tiled=True)
    new_params, new_first, new_second = adam_update(
        expert_params, first_moment, second_moment, grad_shard
    )
    return (trunk_grad, row_loss, new_params, new_first, new_second)


def solution(mesh):
    placed = (
        P(("dp", "expert"), None),
        P(("dp", "expert")),
        P(("dp", "expert"), None),
        P(("dp", "expert"), None),
        P(),
        P("expert", None, None, "dp"),
        P("expert", None, None, "dp"),
        P("expert", None, None, "dp"),
    )
    return jax.shard_map(
        on_device,
        mesh=mesh,
        in_specs=placed,
        out_specs=(
            P(),
            P(("dp", "expert")),
            P("expert", None, None, "dp"),
            P("expert", None, None, "dp"),
            P("expert", None, None, "dp"),
        ),
        check_vma=False,
    )
```

```python
import jax
import jax.numpy as jnp
from jax import lax
from jax.experimental import pallas as pl
from jax.experimental.pallas import tpu as pltpu
from jax.sharding import PartitionSpec as P

MESH = pl.DeviceIdType.MESH
bf16 = jnp.bfloat16
f32 = jnp.float32
i32 = jnp.int32

loss_scale = 1.0 / 32.0
beta_one = 0.9
beta_two = 0.999
learn_rate = 0.05
adam_eps = 1e-08
adam_step = 10

NZ, NY, NC, NX = 8, 4, 2, 4
PLANE = NZ * NY * NC
GROUP = NY * NC
D = 256
ROWS = 1024
CELLS = 2048
CAP = 32
CHUNK = GROUP * CAP
SHARE = 512


def adam_update(params, first, second, grads):
    first_new = beta_one * first + (1.0 - beta_one) * grads
    second_new = beta_two * second + (1.0 - beta_two) * grads * grads
    first_hat = first_new / (1.0 - beta_one**adam_step)
    second_hat = second_new / (1.0 - beta_two**adam_step)
    return (
        params - learn_rate * first_hat / (jnp.sqrt(second_hat) + adam_eps),
        first_new,
        second_new,
    )


def dot(a, b):
    return jnp.dot(a, b, preferred_element_type=f32)


def sigmoid(v):
    return 0.5 + 0.5 * jnp.tanh(0.5 * v)


def onehot(mask):
    return jnp.where(mask, 1.0, 0.0).astype(bf16)


def order_of(t):
    return (4 + (1 - 2 * (t % 2)) * ((t + 1) // 2)) % NZ


def fused(
    table, sidx, region, targets, wt, params,
    gout, loss_out, tg_out,
    send, recv, w, wt_t, g, pay, qrow, place, hbuf, sbuf, tacc,
    rs_s, rs_r, ptile, prx, xr, agb, lsend, lrecv,
    a2a_ss, a2a_rs, ag_ss, ag_rs, l_ss, l_rs, r_ss, r_rs, p_ss, p_rs, x_ss, x_rs, b_ss, b_rs,
):
    me = lax.axis_index("expert")
    mx = lax.axis_index("dp")
    mz = me // GROUP
    my = (me // NC) % NY
    mc = me % NC

    def peer(o):
        return ((mz + o // GROUP) % NZ) * GROUP + ((my + (o // NC) % NY) % NY) * NC + (mc + o % NC) % NC

    def source(o):
        return (
            ((mz + NZ - o // GROUP) % NZ) * GROUP
            + ((my + NY - (o // NC) % NY) % NY) * NC
            + (mc + NC - o % NC) % NC
        )

    def plane_copy(src, dst, ss, rs, to):
        return pltpu.make_async_remote_copy(
            src_ref=src, dst_ref=dst, send_sem=ss, recv_sem=rs,
            device_id={"expert": to}, device_id_type=MESH,
        )

    def dp_copy(src, dst, ss, rs, shift):
        return pltpu.make_async_remote_copy(
            src_ref=src, dst_ref=dst, send_sem=ss, recv_sem=rs,
            device_id={"dp": (mx + shift) % NX}, device_id_type=MESH,
        )

    barrier = pltpu.get_barrier_semaphore()

    @pl.loop(1, PLANE)
    def _(o):
        pl.semaphore_signal(barrier, inc=1, device_id={"expert": peer(o)}, device_id_type=MESH)

    for shift in (1, 2, 3):
        pl.semaphore_signal(
            barrier, inc=1, device_id={"dp": (mx + shift) % NX}, device_id_type=MESH
        )

    w[0] = params[...].astype(bf16)
    pl.semaphore_wait(barrier, PLANE - 1 + NX - 1)

    gather = [
        dp_copy(w.at[0, 0], w.at[3, 0], ag_ss.at[0], ag_rs.at[0], 1),
        dp_copy(w.at[0, 1], w.at[1, 1], ag_ss.at[1], ag_rs.at[1], 3),
        dp_copy(w.at[0, 1], w.at[3, 1], ag_ss.at[2], ag_rs.at[2], 1),
        dp_copy(w.at[0, 0], w.at[1, 0], ag_ss.at[3], ag_rs.at[3], 3),
        dp_copy(w.at[3, 0], w.at[2, 0], ag_ss.at[4], ag_rs.at[4], 1),
        dp_copy(w.at[1, 1], w.at[2, 1], ag_ss.at[5], ag_rs.at[5], 3),
    ]
    for copy in gather[:4]:
        copy.start()

    named = region[...]
    q = (
        (((named >> 3) - mz) & (NZ - 1)) * GROUP
        + ((((named >> 1) & (NY - 1)) - my) & (NY - 1)) * NC
        + (((named & 1) - mc) & (NC - 1))
    )
    qrow[...] = q
    before = onehot(
        lax.broadcasted_iota(i32, (256, 256), 0) < lax.broadcasted_iota(i32, (256, 256), 1)
    )
    carry = jnp.zeros((PLANE, 1), f32)
    for b in range(ROWS // 256):
        part = q[:, 256 * b : 256 * b + 256]
        hot = jnp.where(lax.broadcasted_iota(i32, (PLANE, 256), 0) == part, 1.0, 0.0)
        count = dot(hot.astype(bf16), before) + carry
        slot = jnp.sum(hot * count, axis=0, keepdims=True)
        carry = carry + jnp.sum(hot, axis=1, keepdims=True)
        place[:, 256 * b : 256 * b + 256] = part * CAP + slot.astype(i32)

    for b in range(ROWS // 256):
        cols = [
            jnp.transpose(
                jnp.broadcast_to(
                    sidx[:, 256 * b + 128 * h : 256 * b + 128 * h + 128].astype(f32), (128, 128)
                )
            )
            for h in range(2)
        ]
        col = jnp.concatenate(cols, axis=0).astype(i32)
        wide = jnp.concatenate([col] * (CELLS // 128), axis=1)
        pick = onehot(wide == lax.broadcasted_iota(i32, (256, CELLS), 1))
        pay[256 * b : 256 * b + 256, :D] = dot(pick, table[...]).astype(bf16)
    pay[:, D:] = targets[...]

    @pl.loop(0, NZ)
    def _(t):
        dz = order_of(t)
        base = pl.multiple_of(dz * CHUNK, CHUNK)
        mask = lax.broadcasted_iota(i32, (CHUNK, ROWS), 0) + base == place[...]
        send[pl.ds(base, CHUNK), :] = dot(onehot(mask), pay[...]).astype(bf16)

        @pl.loop(0, GROUP)
        def _(i):
            o = dz * GROUP + i

            @pl.when(o != 0)
            def _():
                rows = pl.ds(pl.multiple_of(o * CAP, CAP), CAP)
                plane_copy(
                    send.at[rows], recv.at[rows], a2a_ss.at[dz], a2a_rs.at[dz], peer(o)
                ).start()

    recv[0:CAP, :] = send[0:CAP, :]
    g[...] = jnp.zeros_like(g)
    tacc[...] = jnp.zeros_like(tacc)

    def flip(k, m):
        wt_t[k, m] = jnp.transpose(w[k, m])

    gather[0].wait_recv()
    gather[4].start()
    gather[1].wait_recv()
    gather[5].start()
    flip(0, 0)
    flip(0, 1)
    flip(3, 0)
    flip(1, 1)
    gather[2].wait_recv()
    flip(3, 1)
    gather[3].wait_recv()
    flip(1, 0)
    gather[4].wait_recv()
    flip(2, 0)
    gather[5].wait_recv()
    flip(2, 1)

    reduce = [
        dp_copy(rs_s.at[n], rs_r.at[n], r_ss.at[n], r_rs.at[n], 1 if n in (0, 2, 4) else 3)
        for n in range(6)
    ]

    def chunk_wait(dz):
        @pl.when(dz != 0)
        def _():
            rows = pl.ds(pl.multiple_of(dz * CHUNK, CHUNK), CHUNK)
            plane_copy(send.at[rows], recv.at[rows], a2a_ss.at[dz], a2a_rs.at[dz], me).wait_recv()

        @pl.when(dz == 0)
        def _():
            rows = pl.ds(CAP, CHUNK - CAP)
            plane_copy(send.at[rows], recv.at[rows], a2a_ss.at[0], a2a_rs.at[0], me).wait_recv()

    @pl.loop(0, NZ)
    def _(t):
        dz = order_of(t)
        chunk_wait(dz)
        rows = pl.ds(pl.multiple_of(dz * CHUNK, CHUNK), CHUNK)
        feats = recv[rows, :D]
        feats_f = feats.astype(f32)
        trunk_pre = dot(feats, wt[...])
        trunk_sig = sigmoid(trunk_pre)
        trunk_f = feats_f + trunk_pre * trunk_sig
        trunk_out = trunk_f.astype(bf16)
        trunk_t = jnp.transpose(trunk_f).astype(bf16)
        predicted = jnp.zeros((CHUNK, D), f32)
        for k in range(NX):
            up = dot(trunk_out, w[k, 0])
            sig = sigmoid(up)
            hid = up * sig
            hid_b = hid.astype(bf16)
            hbuf[k] = hid_b
            sbuf[k] = sig + hid * (1.0 - sig)
            predicted = predicted + dot(hid_b, wt_t[k, 1])
        errors = predicted - recv[rows, D:].astype(f32)
        squares = errors * errors
        squares = jnp.transpose(squares[:, :128] + squares[:, 128:])
        lsend[dz] = jnp.sum(squares, axis=0, keepdims=True) * (0.5 * loss_scale)

        @pl.loop(0, GROUP)
        def _(i):
            o = dz * GROUP + i

            @pl.when(o != 0)
            def _():
                plane_copy(lsend.at[dz], lrecv.at[o], l_ss, l_rs, source(o)).start()

        scaled_f = errors * loss_scale
        scaled = scaled_f.astype(bf16)
        scaled_t = jnp.transpose(scaled_f).astype(bf16)
        row_grad = jnp.zeros((CHUNK, D), f32)
        for k in (2, 1, 3, 0):
            pre_grad = (dot(scaled, w[k, 1]) * sbuf[k]).astype(bf16)
            g[k, 0] += dot(trunk_t, pre_grad)
            g[k, 1] += dot(scaled_t, hbuf[k])
            if k:

                @pl.when(t == NZ - 1)
                def _():
                    for n, m in {2: ((0, 0), (1, 1)), 1: ((2, 1),), 3: ((3, 0),)}[k]:
                        rs_s[n] = g[k, m].astype(bf16)
                        reduce[n].start()

            row_grad = row_grad + dot(pre_grad, wt_t[k, 0])
        slope = trunk_sig + trunk_pre * trunk_sig * (1.0 - trunk_sig)
        trunk_slope = (row_grad.astype(bf16).astype(f32) * slope).astype(bf16)
        tacc[...] += dot(jnp.transpose(feats_f).astype(bf16), trunk_slope)

    for p in range(PLANE):
        ptile[p] = tacc[8 * (p % 32) : 8 * (p % 32) + 8, 128 * (p // 32) : 128 * (p // 32) + 128]

    @pl.loop(1, PLANE)
    def _(o):
        to = peer(o)
        plane_copy(ptile.at[to], prx.at[o], p_ss, p_rs, to).start()

    prx[0] = ptile[me]
    lrecv[0] = lsend[0]

    reduce[0].wait_recv()
    rs_s[4] = (g[1, 0] + rs_r[0].astype(f32)).astype(bf16)
    reduce[4].start()
    reduce[1].wait_recv()
    rs_s[5] = (g[3, 1] + rs_r[1].astype(f32)).astype(bf16)
    reduce[5].start()

    others = pl.ds(1, PLANE - 1)
    plane_copy(ptile.at[others], prx.at[others], p_ss, p_rs, me).wait_recv()
    xr[mx] = jnp.sum(prx[...], axis=0)
    for shift in (1, 2, 3):
        dp_copy(xr.at[mx], xr.at[mx], x_ss, x_rs, shift).start()

    plane_copy(lrecv.at[others], lrecv.at[others], l_ss, l_rs, me).wait_recv()
    table_f = lrecv[...].reshape(PLANE, CHUNK)
    high = table_f.astype(bf16)
    rest = table_f - high.astype(f32)
    middle = rest.astype(bf16)
    low = (rest - middle.astype(f32)).astype(bf16)
    spot = place[...] & (CHUNK - 1)
    hot = onehot(lax.broadcasted_iota(i32, (PLANE, ROWS), 0) == qrow[...])
    seen = sum(
        lax.dot_general(part, hot, (((0,), (0,)), ((), ())), preferred_element_type=f32)
        for part in (high, middle, low)
    )
    loss_out[...] = jnp.sum(
        jnp.where(lax.broadcasted_iota(i32, (CHUNK, ROWS), 0) == spot, seen, 0.0),
        axis=0,
        keepdims=True,
    )

    three = pl.ds(0, NX - 1)
    dp_copy(xr.at[three], xr.at[three], x_ss, x_rs, 1).wait_recv()
    agb[me] = (xr[0] + xr[1]) + (xr[2] + xr[3])

    @pl.loop(1, PLANE)
    def _(o):
        plane_copy(agb.at[me], agb.at[me], b_ss, b_rs, peer(o)).start()

    reduce[2].wait_recv()
    reduce[3].wait_recv()
    reduce[4].wait_recv()
    gout[0] = g[0, 0] + rs_r[3].astype(f32) + rs_r[4].astype(f32)
    reduce[5].wait_recv()
    gout[1] = g[0, 1] + rs_r[2].astype(f32) + rs_r[5].astype(f32)

    plane_copy(agb.at[others], agb.at[others], b_ss, b_rs, me).wait_recv()
    for p in range(PLANE):
        tg_out[8 * (p % 32) : 8 * (p % 32) + 8, 128 * (p // 32) : 128 * (p // 32) + 128] = agb[p]

    for dz in range(NZ):
        rows = pl.ds(CAP if dz == 0 else dz * CHUNK, CHUNK - CAP if dz == 0 else CHUNK)
        plane_copy(send.at[rows], recv.at[rows], a2a_ss.at[dz], a2a_rs.at[dz], me).wait_send()
    for copy in gather + reduce:
        copy.wait_send()
    plane_copy(lrecv.at[others], lrecv.at[others], l_ss, l_rs, me).wait_send()
    plane_copy(ptile.at[others], prx.at[others], p_ss, p_rs, me).wait_send()
    plane_copy(agb.at[others], agb.at[others], b_ss, b_rs, me).wait_send()
    dp_copy(xr.at[three], xr.at[three], x_ss, x_rs, 1).wait_send()


def on_device(
    cell_table, sample_index, region, targets, trunk_weight, expert_params, first_moment, second_moment
):
    vmem = pl.BlockSpec(memory_space=pltpu.VMEM)
    dma = pltpu.SemaphoreType.DMA
    grads, losses, trunk_grad = pl.pallas_call(
        fused,
        out_shape=(
            jax.ShapeDtypeStruct((2, D, SHARE), f32),
            jax.ShapeDtypeStruct((1, ROWS), f32),
            jax.ShapeDtypeStruct((D, D), f32),
        ),
        in_specs=[vmem] * 6,
        out_specs=(vmem, vmem, vmem),
        scratch_shapes=[
            pltpu.VMEM((PLANE * CAP, 2 * D), bf16),
            pltpu.VMEM((PLANE * CAP, 2 * D), bf16),
            pltpu.VMEM((NX, 2, D, SHARE), bf16),
            pltpu.VMEM((NX, 2, SHARE, D), bf16),
            pltpu.VMEM((NX, 2, D, SHARE), f32),
            pltpu.VMEM((ROWS, 2 * D), bf16),
            pltpu.VMEM((1, ROWS), i32),
            pltpu.VMEM((1, ROWS), i32),
            pltpu.VMEM((NX, CHUNK, SHARE), bf16),
            pltpu.VMEM((NX, CHUNK, SHARE), f32),
            pltpu.VMEM((D, D), f32),
            pltpu.VMEM((6, D, SHARE), bf16),
            pltpu.VMEM((6, D, SHARE), bf16),
            pltpu.VMEM((PLANE, 8, 128), f32),
            pltpu.VMEM((PLANE, 8, 128), f32),
            pltpu.VMEM((NX, 8, 128), f32),
            pltpu.VMEM((PLANE, 8, 128), f32),
            pltpu.VMEM((NZ, 1, CHUNK), f32),
            pltpu.VMEM((PLANE, 1, CHUNK), f32),
            dma((NZ,)), dma((NZ,)),
            dma((6,)), dma((6,)),
            dma, dma,
            dma((6,)), dma((6,)),
            dma, dma,
            dma, dma,
            dma, dma,
        ],
        compiler_params=pltpu.CompilerParams(
            collective_id=0, has_side_effects=True, vmem_limit_bytes=56 << 20
        ),
        name="fused_step",
    )(
        cell_table,
        sample_index.reshape(1, ROWS),
        region.reshape(1, ROWS),
        targets,
        trunk_weight,
        expert_params[0],
    )
    new_params, new_first, new_second = adam_update(
        expert_params, first_moment, second_moment, grads[None]
    )
    return (trunk_grad, losses.reshape(ROWS), new_params, new_first, new_second)


def solution(mesh):
    placed = (
        P(("dp", "expert"), None),
        P(("dp", "expert")),
        P(("dp", "expert"), None),
        P(("dp", "expert"), None),
        P(),
        P("expert", None, None, "dp"),
        P("expert", None, None, "dp"),
        P("expert", None, None, "dp"),
    )
    return jax.shard_map(
        on_device,
        mesh=mesh,
        in_specs=placed,
        out_specs=(
            P(),
            P(("dp", "expert")),
            P("expert", None, None, "dp"),
            P("expert", None, None, "dp"),
            P("expert", None, None, "dp"),
        ),
        check_vma=False,
    )
```

```python
import jax
import jax.numpy as jnp
from jax import lax
from jax.experimental import pallas as pl
from jax.experimental.pallas import tpu as pltpu
from jax.sharding import PartitionSpec as P

MESH = pl.DeviceIdType.MESH
bf16 = jnp.bfloat16
f32 = jnp.float32
i32 = jnp.int32

loss_scale = 1.0 / 32.0
beta_one = 0.9
beta_two = 0.999
learn_rate = 0.05
adam_eps = 1e-08
adam_step = 10

NZ, NY, NC, NX = 8, 4, 2, 4
PLANE = NZ * NY * NC
GROUP = NY * NC
D = 256
ROWS = 1024
CELLS = 2048
CAP = 32
CHUNK = GROUP * CAP
SHARE = 512


def adam_update(params, first, second, grads):
    first_new = beta_one * first + (1.0 - beta_one) * grads
    second_new = beta_two * second + (1.0 - beta_two) * grads * grads
    first_hat = first_new / (1.0 - beta_one**adam_step)
    second_hat = second_new / (1.0 - beta_two**adam_step)
    return (
        params - learn_rate * first_hat / (jnp.sqrt(second_hat) + adam_eps),
        first_new,
        second_new,
    )


def dot(a, b):
    return jnp.dot(a, b, preferred_element_type=f32)


def sigmoid(v):
    return 0.5 + 0.5 * jnp.tanh(0.5 * v)


def onehot(mask):
    return jnp.where(mask, 1.0, 0.0).astype(bf16)


def fused(
    table, sidx, region, targets, wt, params,
    gout, loss_out, tg_out,
    send, recv, w, wt_t, g, pay, qrow, place, hbuf, sbuf, pbuf, tacc,
    rs_s, rs_r, tr, tz, zr, xr, agz, agb, lsend, lmid, lrecv,
    a_ss, a_rs, ready, ag_ss, ag_rs, r_ss, r_rs, s_ss, s_rs,
):
    me = lax.axis_index("expert")
    mx = lax.axis_index("dp")
    mz = me // GROUP
    my = (me // NC) % NY
    mc = me % NC
    mg = me % GROUP

    def along_z(d):
        return ((mz + d) % NZ) * GROUP + mg

    def in_group(i):
        return mz * GROUP + ((my + i // NC) % NY) * NC + (mc + i % NC) % NC

    def before_in_group(i):
        return mz * GROUP + ((my + NY - i // NC) % NY) * NC + (mc + NC - i % NC) % NC

    def owner(i, d):
        return ((mz + d) % NZ) * GROUP + ((my + i // NC) % NY) * NC + (mc + i % NC) % NC

    def plane_copy(src, dst, ss, rs, to):
        return pltpu.make_async_remote_copy(
            src_ref=src, dst_ref=dst, send_sem=ss, recv_sem=rs,
            device_id={"expert": to}, device_id_type=MESH,
        )

    def dp_copy(src, dst, ss, rs, shift):
        return pltpu.make_async_remote_copy(
            src_ref=src, dst_ref=dst, send_sem=ss, recv_sem=rs,
            device_id={"dp": (mx + shift) % NX}, device_id_type=MESH,
        )

    barrier = pltpu.get_barrier_semaphore()
    for d in (4, 3, 5, 2, 6, 1, 7):
        pl.semaphore_signal(barrier, inc=1, device_id={"expert": along_z(d)}, device_id_type=MESH)
    for i in range(1, GROUP):
        pl.semaphore_signal(barrier, inc=1, device_id={"expert": in_group(i)}, device_id_type=MESH)
    for shift in (1, 2, 3):
        pl.semaphore_signal(
            barrier, inc=1, device_id={"dp": (mx + shift) % NX}, device_id_type=MESH
        )

    w[0] = params[...].astype(bf16)

    named = region[...]
    q = (
        ((((named >> 1) & (NY - 1)) - my) & (NY - 1)) * NC * NZ
        + (((named & 1) - mc) & (NC - 1)) * NZ
        + (((named >> 3) - mz) & (NZ - 1))
    )
    qrow[...] = q
    before = onehot(
        lax.broadcasted_iota(i32, (256, 256), 0) < lax.broadcasted_iota(i32, (256, 256), 1)
    )
    carry = jnp.zeros((PLANE, 1), f32)
    for b in range(ROWS // 256):
        part = q[:, 256 * b : 256 * b + 256]
        hot = jnp.where(lax.broadcasted_iota(i32, (PLANE, 256), 0) == part, 1.0, 0.0)
        count = dot(hot.astype(bf16), before) + carry
        slot = jnp.sum(hot * count, axis=0, keepdims=True)
        carry = carry + jnp.sum(hot, axis=1, keepdims=True)
        place[:, 256 * b : 256 * b + 256] = part * CAP + slot.astype(i32)

    for b in range(ROWS // 256):
        cols = [
            jnp.transpose(
                jnp.broadcast_to(
                    sidx[:, 256 * b + 128 * h : 256 * b + 128 * h + 128].astype(f32), (128, 128)
                )
            )
            for h in range(2)
        ]
        col = jnp.concatenate(cols, axis=0).astype(i32)
        wide = jnp.concatenate([col] * (CELLS // 128), axis=1)
        pick = onehot(wide == lax.broadcasted_iota(i32, (256, CELLS), 1))
        pay[256 * b : 256 * b + 256, :D] = dot(pick, table[...]).astype(bf16)
    pay[:, D:] = targets[...]

    def pack(i):
        mask = lax.broadcasted_iota(i32, (CHUNK, ROWS), 0) + i * CHUNK == place[...]
        send[i] = dot(onehot(mask), pay[...]).astype(bf16)

    def row_copy(i, d):
        rows = pl.ds(d * CAP, CAP)
        return plane_copy(
            send.at[i, rows], recv.at[i, rows], a_ss.at[i], a_rs.at[i], owner(i, d)
        )

    pack(0)
    recv[0, 0:CAP] = send[0, 0:CAP]
    pl.semaphore_wait(barrier, NZ - 1 + GROUP - 1 + NX - 1)
    for d in (4, 3, 5, 2, 6, 1, 7):
        row_copy(0, d).start()

    for i in range(1, GROUP):
        pl.semaphore_signal(ready, inc=1, device_id={"expert": in_group(i)}, device_id_type=MESH)

    gather = [
        dp_copy(w.at[0, 0], w.at[3, 0], ag_ss.at[0], ag_rs.at[0], 1),
        dp_copy(w.at[0, 1], w.at[1, 1], ag_ss.at[1], ag_rs.at[1], 3),
        dp_copy(w.at[0, 1], w.at[3, 1], ag_ss.at[2], ag_rs.at[2], 1),
        dp_copy(w.at[0, 0], w.at[1, 0], ag_ss.at[3], ag_rs.at[3], 3),
        dp_copy(w.at[3, 0], w.at[2, 0], ag_ss.at[4], ag_rs.at[4], 1),
        dp_copy(w.at[1, 1], w.at[2, 1], ag_ss.at[5], ag_rs.at[5], 3),
    ]
    for copy in gather[:4]:
        copy.start()

    pack(1)
    pl.semaphore_wait(ready, GROUP - 1)

    @pl.loop(1, GROUP)
    def _(i):
        for d in (4, 3, 5, 2, 6, 1, 7, 0):
            row_copy(i, d).start()

        @pl.when(i < GROUP - 1)
        def _():
            pack(i + 1)

    g[...] = jnp.zeros_like(g)
    tacc[...] = jnp.zeros_like(tacc)

    def flip(k, m):
        wt_t[k, m] = jnp.transpose(w[k, m])

    gather[0].wait_recv()
    gather[4].start()
    gather[1].wait_recv()
    gather[5].start()
    flip(0, 0)
    flip(0, 1)
    flip(3, 0)
    flip(1, 1)
    gather[2].wait_recv()
    flip(3, 1)
    gather[3].wait_recv()
    flip(1, 0)
    gather[4].wait_recv()
    flip(2, 0)
    gather[5].wait_recv()
    flip(2, 1)

    reduce = [
        dp_copy(rs_s.at[n], rs_r.at[n], r_ss.at[n], r_rs.at[n], 1 if n in (0, 2, 4) else 3)
        for n in range(6)
    ]
    others = pl.ds(1, GROUP - 1)
    rest = pl.ds(CAP, CHUNK - CAP)

    @pl.loop(0, GROUP)
    def _(t):
        @pl.when(t == 0)
        def _():
            plane_copy(send.at[0, rest], recv.at[0, rest], a_ss.at[0], a_rs.at[0], me).wait_recv()

        @pl.when(t != 0)
        def _():
            plane_copy(send.at[t], recv.at[t], a_ss.at[t], a_rs.at[t], me).wait_recv()

        feats = recv[t, :, :D]
        feats_f = feats.astype(f32)
        trunk_pre = dot(feats, wt[...])
        trunk_sig = sigmoid(trunk_pre)
        trunk_f = feats_f + trunk_pre * trunk_sig
        trunk_out = trunk_f.astype(bf16)
        trunk_t = jnp.transpose(trunk_f).astype(bf16)
        predicted = jnp.zeros((CHUNK, D), f32)
        for k in range(NX):
            up = dot(trunk_out, w[k, 0])
            sig = sigmoid(up)
            hid = up * sig
            hid_b = hid.astype(bf16)
            hbuf[k] = hid_b
            sbuf[k] = sig + hid * (1.0 - sig)
            predicted = predicted + dot(hid_b, wt_t[k, 1])
        errors = predicted - recv[t, :, D:].astype(f32)
        squares = errors * errors
        squares = jnp.transpose(squares[:, :128] + squares[:, 128:])
        lsend[t] = jnp.sum(squares, axis=0, keepdims=True) * (0.5 * loss_scale)

        @pl.when(t != 0)
        def _():
            plane_copy(
                lsend.at[t], lmid.at[t], s_ss.at[0], s_rs.at[0], before_in_group(t)
            ).start()

        scaled_f = errors * loss_scale
        scaled = scaled_f.astype(bf16)
        scaled_t = jnp.transpose(scaled_f).astype(bf16)
        row_grad = jnp.zeros((CHUNK, D), f32)
        for k in range(NX):
            pre_grad = (dot(scaled, w[k, 1]) * sbuf[k]).astype(bf16)
            pbuf[k] = pre_grad
            row_grad = row_grad + dot(pre_grad, wt_t[k, 0])
        slope = trunk_sig + trunk_pre * trunk_sig * (1.0 - trunk_sig)
        trunk_slope = (row_grad.astype(bf16).astype(f32) * slope).astype(bf16)
        tacc[...] += dot(jnp.transpose(feats_f).astype(bf16), trunk_slope)

        @pl.when(t == GROUP - 1)
        def _():
            for i in range(1, GROUP):
                to = in_group(i)
                share = pl.ds(pl.multiple_of((to % GROUP) * 32, 32), 32)
                plane_copy(tacc.at[share], tr.at[i], s_ss.at[1], s_rs.at[1], to).start()

        for k in (2, 1, 3, 0):
            g[k, 0] += dot(trunk_t, pbuf[k])
            g[k, 1] += dot(scaled_t, hbuf[k])
            if k:

                @pl.when(t == GROUP - 1)
                def _():
                    for n, m in {2: ((0, 0), (1, 1)), 1: ((2, 1),), 3: ((3, 0),)}[k]:
                        rs_s[n] = g[k, m].astype(bf16)
                        reduce[n].start()

    tr[0] = tacc[pl.ds(pl.multiple_of(mg * 32, 32), 32)]
    lmid[0] = lsend[0]
    plane_copy(tr.at[others], tr.at[others], s_ss.at[1], s_rs.at[1], me).wait_recv()
    total = jnp.sum(tr[...], axis=0)
    for p in range(NZ):
        tz[p] = total[8 * (p % 4) : 8 * (p % 4) + 8, 128 * (p // 4) : 128 * (p // 4) + 128]
    for d in (4, 3, 5, 2, 6, 1, 7):
        plane_copy(tz.at[(mz + d) % NZ], zr.at[d], s_ss.at[2], s_rs.at[2], along_z(d)).start()
    zr[0] = tz[mz]

    plane_copy(lmid.at[others], lmid.at[others], s_ss.at[0], s_rs.at[0], me).wait_recv()
    for d in (4, 3, 5, 2, 6, 1, 7):
        plane_copy(lmid, lrecv.at[d], s_ss.at[3], s_rs.at[3], along_z(NZ - d)).start()
    lrecv[0] = lmid[...]

    reduce[0].wait_recv()
    rs_s[4] = (g[1, 0] + rs_r[0].astype(f32)).astype(bf16)
    reduce[4].start()
    reduce[1].wait_recv()
    rs_s[5] = (g[3, 1] + rs_r[1].astype(f32)).astype(bf16)
    reduce[5].start()

    plane_copy(zr.at[others], zr.at[others], s_ss.at[2], s_rs.at[2], me).wait_recv()
    xr[mx] = jnp.sum(zr[...], axis=0)
    for shift in (1, 2, 3):
        dp_copy(xr.at[mx], xr.at[mx], s_ss.at[4], s_rs.at[4], shift).start()

    three = pl.ds(0, NX - 1)
    dp_copy(xr.at[three], xr.at[three], s_ss.at[4], s_rs.at[4], 1).wait_recv()
    agz[mz] = (xr[0] + xr[1]) + (xr[2] + xr[3])
    for d in (4, 3, 5, 2, 6, 1, 7):
        plane_copy(agz.at[mz], agz.at[mz], s_ss.at[5], s_rs.at[5], along_z(d)).start()

    plane_copy(lrecv.at[others], lrecv.at[others], s_ss.at[3], s_rs.at[3], me).wait_recv()
    table_f = lrecv[...].reshape(PLANE, CHUNK)
    high = table_f.astype(bf16)
    left = table_f - high.astype(f32)
    middle = left.astype(bf16)
    low = (left - middle.astype(f32)).astype(bf16)
    spot = place[...] & (CHUNK - 1)
    turned = (qrow[...] & (NZ - 1)) * GROUP + (qrow[...] >> 3)
    hot = onehot(lax.broadcasted_iota(i32, (PLANE, ROWS), 0) == turned)
    seen = sum(
        lax.dot_general(part, hot, (((0,), (0,)), ((), ())), preferred_element_type=f32)
        for part in (high, middle, low)
    )
    loss_out[...] = jnp.sum(
        jnp.where(lax.broadcasted_iota(i32, (CHUNK, ROWS), 0) == spot, seen, 0.0),
        axis=0,
        keepdims=True,
    )

    plane_copy(agz.at[others], agz.at[others], s_ss.at[5], s_rs.at[5], me).wait_recv()
    for i in range(1, GROUP):
        plane_copy(agz, agb.at[mg], s_ss.at[6], s_rs.at[6], in_group(i)).start()
    agb[mg] = agz[...]

    reduce[2].wait_recv()
    reduce[3].wait_recv()
    reduce[4].wait_recv()
    gout[0] = g[0, 0] + rs_r[3].astype(f32) + rs_r[4].astype(f32)
    reduce[5].wait_recv()
    gout[1] = g[0, 1] + rs_r[2].astype(f32) + rs_r[5].astype(f32)

    plane_copy(agb.at[others], agb.at[others], s_ss.at[6], s_rs.at[6], me).wait_recv()
    for i in range(GROUP):
        for p in range(NZ):
            row, col = 32 * i + 8 * (p % 4), 128 * (p // 4)
            tg_out[row : row + 8, col : col + 128] = agb[i, p]

    plane_copy(send.at[0, rest], recv.at[0, rest], a_ss.at[0], a_rs.at[0], me).wait_send()
    for i in range(1, GROUP):
        plane_copy(send.at[i], recv.at[i], a_ss.at[i], a_rs.at[i], me).wait_send()
    for copy in gather + reduce:
        copy.wait_send()
    for n, ref in ((0, lmid), (1, tr), (2, zr), (3, lrecv), (5, agz), (6, agb)):
        plane_copy(ref.at[others], ref.at[others], s_ss.at[n], s_rs.at[n], me).wait_send()
    dp_copy(xr.at[three], xr.at[three], s_ss.at[4], s_rs.at[4], 1).wait_send()


def on_device(
    cell_table, sample_index, region, targets, trunk_weight, expert_params, first_moment, second_moment
):
    vmem = pl.BlockSpec(memory_space=pltpu.VMEM)
    dma = pltpu.SemaphoreType.DMA
    grads, losses, trunk_grad = pl.pallas_call(
        fused,
        out_shape=(
            jax.ShapeDtypeStruct((2, D, SHARE), f32),
            jax.ShapeDtypeStruct((1, ROWS), f32),
            jax.ShapeDtypeStruct((D, D), f32),
        ),
        in_specs=[vmem] * 6,
        out_specs=(vmem, vmem, vmem),
        scratch_shapes=[
            pltpu.VMEM((GROUP, CHUNK, 2 * D), bf16),
            pltpu.VMEM((GROUP, CHUNK, 2 * D), bf16),
            pltpu.VMEM((NX, 2, D, SHARE), bf16),
            pltpu.VMEM((NX, 2, SHARE, D), bf16),
            pltpu.VMEM((NX, 2, D, SHARE), f32),
            pltpu.VMEM((ROWS, 2 * D), bf16),
            pltpu.VMEM((1, ROWS), i32),
            pltpu.VMEM((1, ROWS), i32),
            pltpu.VMEM((NX, CHUNK, SHARE), bf16),
            pltpu.VMEM((NX, CHUNK, SHARE), f32),
            pltpu.VMEM((NX, CHUNK, SHARE), bf16),
            pltpu.VMEM((D, D), f32),
            pltpu.VMEM((6, D, SHARE), bf16),
            pltpu.VMEM((6, D, SHARE), bf16),
            pltpu.VMEM((GROUP, 32, D), f32),
            pltpu.VMEM((NZ, 8, 128), f32),
            pltpu.VMEM((NZ, 8, 128), f32),
            pltpu.VMEM((NX, 8, 128), f32),
            pltpu.VMEM((NZ, 8, 128), f32),
            pltpu.VMEM((GROUP, NZ, 8, 128), f32),
            pltpu.VMEM((NZ, 1, CHUNK), f32),
            pltpu.VMEM((NZ, 1, CHUNK), f32),
            pltpu.VMEM((GROUP, NZ, 1, CHUNK), f32),
            dma((GROUP,)), dma((GROUP,)), pltpu.SemaphoreType.REGULAR,
            dma((6,)), dma((6,)),
            dma((6,)), dma((6,)),
            dma((7,)), dma((7,)),
        ],
        compiler_params=pltpu.CompilerParams(
            collective_id=0, has_side_effects=True, vmem_limit_bytes=56 << 20
        ),
        name="fused_step",
    )(
        cell_table,
        sample_index.reshape(1, ROWS),
        region.reshape(1, ROWS),
        targets,
        trunk_weight,
        expert_params[0],
    )
    new_params, new_first, new_second = adam_update(
        expert_params, first_moment, second_moment, grads[None]
    )
    return (trunk_grad, losses.reshape(ROWS), new_params, new_first, new_second)


def solution(mesh):
    placed = (
        P(("dp", "expert"), None),
        P(("dp", "expert")),
        P(("dp", "expert"), None),
        P(("dp", "expert"), None),
        P(),
        P("expert", None, None, "dp"),
        P("expert", None, None, "dp"),
        P("expert", None, None, "dp"),
    )
    return jax.shard_map(
        on_device,
        mesh=mesh,
        in_specs=placed,
        out_specs=(
            P(),
            P(("dp", "expert")),
            P("expert", None, None, "dp"),
            P("expert", None, None, "dp"),
            P("expert", None, None, "dp"),
        ),
        check_vma=False,
    )
```

```python
import jax
import jax.numpy as jnp
from jax import lax
from jax.experimental import pallas as pl
from jax.experimental.pallas import tpu as pltpu
from jax.sharding import PartitionSpec as P

MESH = pl.DeviceIdType.MESH
bf16 = jnp.bfloat16
f32 = jnp.float32
i32 = jnp.int32

loss_scale = 1.0 / 32.0
beta_one = 0.9
beta_two = 0.999
learn_rate = 0.05
adam_eps = 1e-08
adam_step = 10

NZ, NY, NC, NX = 8, 4, 2, 4
PLANE = NZ * NY * NC
GROUP = NY * NC
D = 256
ROWS = 1024
CELLS = 2048
CAP = 32
CHUNK = GROUP * CAP
SHARE = 512


def adam_update(params, first, second, grads):
    first_new = beta_one * first + (1.0 - beta_one) * grads
    second_new = beta_two * second + (1.0 - beta_two) * grads * grads
    first_hat = first_new / (1.0 - beta_one**adam_step)
    second_hat = second_new / (1.0 - beta_two**adam_step)
    return (
        params - learn_rate * first_hat / (jnp.sqrt(second_hat) + adam_eps),
        first_new,
        second_new,
    )


def dot(a, b):
    return jnp.dot(a, b, preferred_element_type=f32)


def sigmoid(v):
    return 0.5 + 0.5 * jnp.tanh(0.5 * v)


def onehot(mask):
    return jnp.where(mask, 1.0, 0.0).astype(bf16)


def fused(
    table, sidx, region, targets, wt, params,
    gout, loss_out, tg_out,
    send, recv, w, wt_t, g, pay, qrow, place, hbuf, sbuf, pbuf, tacc,
    rs_s, rs_r, tr, tz, zr, xr, agz, agb, lsend, lmid, lrecv,
    a_ss, a_rs, ready, ag_ss, ag_rs, r_ss, r_rs, s_ss, s_rs,
):
    me = lax.axis_index("expert")
    mx = lax.axis_index("dp")
    mz = me // GROUP
    my = (me // NC) % NY
    mc = me % NC
    mg = me % GROUP

    def along_z(d):
        return ((mz + d) % NZ) * GROUP + mg

    def in_group(i):
        return mz * GROUP + ((my + i // NC) % NY) * NC + (mc + i % NC) % NC

    def before_in_group(i):
        return mz * GROUP + ((my + NY - i // NC) % NY) * NC + (mc + NC - i % NC) % NC

    def owner(i, d):
        return ((mz + d) % NZ) * GROUP + ((my + i // NC) % NY) * NC + (mc + i % NC) % NC

    def plane_copy(src, dst, ss, rs, to):
        return pltpu.make_async_remote_copy(
            src_ref=src, dst_ref=dst, send_sem=ss, recv_sem=rs,
            device_id={"expert": to}, device_id_type=MESH,
        )

    def dp_copy(src, dst, ss, rs, shift):
        return pltpu.make_async_remote_copy(
            src_ref=src, dst_ref=dst, send_sem=ss, recv_sem=rs,
            device_id={"dp": (mx + shift) % NX}, device_id_type=MESH,
        )

    barrier = pltpu.get_barrier_semaphore()
    for d in (4, 3, 5, 2, 6, 1, 7):
        pl.semaphore_signal(barrier, inc=1, device_id={"expert": along_z(d)}, device_id_type=MESH)
    for i in range(1, GROUP):
        pl.semaphore_signal(barrier, inc=1, device_id={"expert": in_group(i)}, device_id_type=MESH)
    for shift in (1, 2, 3):
        pl.semaphore_signal(
            barrier, inc=1, device_id={"dp": (mx + shift) % NX}, device_id_type=MESH
        )

    w[0] = params[...].astype(bf16)

    named = region[...]
    q = (
        ((((named >> 1) & (NY - 1)) - my) & (NY - 1)) * NC * NZ
        + (((named & 1) - mc) & (NC - 1)) * NZ
        + (((named >> 3) - mz) & (NZ - 1))
    )
    qrow[...] = q
    before = onehot(
        lax.broadcasted_iota(i32, (256, 256), 0) < lax.broadcasted_iota(i32, (256, 256), 1)
    )
    carry = jnp.zeros((PLANE, 1), f32)
    for b in range(ROWS // 256):
        part = q[:, 256 * b : 256 * b + 256]
        hot = jnp.where(lax.broadcasted_iota(i32, (PLANE, 256), 0) == part, 1.0, 0.0)
        count = dot(hot.astype(bf16), before) + carry
        slot = jnp.sum(hot * count, axis=0, keepdims=True)
        carry = carry + jnp.sum(hot, axis=1, keepdims=True)
        place[:, 256 * b : 256 * b + 256] = part * CAP + slot.astype(i32)

    for b in range(ROWS // 256):
        cols = [
            jnp.transpose(
                jnp.broadcast_to(
                    sidx[:, 256 * b + 128 * h : 256 * b + 128 * h + 128].astype(f32), (128, 128)
                )
            )
            for h in range(2)
        ]
        col = jnp.concatenate(cols, axis=0).astype(i32)
        wide = jnp.concatenate([col] * (CELLS // 128), axis=1)
        pick = onehot(wide == lax.broadcasted_iota(i32, (256, CELLS), 1))
        pay[256 * b : 256 * b + 256, :D] = dot(pick, table[...]).astype(bf16)
    pay[:, D:] = targets[...]

    def pack(i):
        mask = lax.broadcasted_iota(i32, (CHUNK, ROWS), 0) + i * CHUNK == place[...]
        send[i] = dot(onehot(mask), pay[...]).astype(bf16)

    def row_copy(i, d):
        rows = pl.ds(d * CAP, CAP)
        return plane_copy(
            send.at[i, rows], recv.at[i, rows], a_ss.at[i], a_rs.at[i], owner(i, d)
        )

    pack(0)
    recv[0, 0:CAP] = send[0, 0:CAP]
    pl.semaphore_wait(barrier, NZ - 1 + GROUP - 1 + NX - 1)
    for d in (4, 3, 5, 2, 6, 1, 7):
        row_copy(0, d).start()

    for i in range(1, GROUP):
        pl.semaphore_signal(ready, inc=1, device_id={"expert": in_group(i)}, device_id_type=MESH)

    gather = [
        dp_copy(w.at[0, 0], w.at[3, 0], ag_ss.at[0], ag_rs.at[0], 1),
        dp_copy(w.at[0, 1], w.at[1, 1], ag_ss.at[1], ag_rs.at[1], 3),
        dp_copy(w.at[0, 1], w.at[3, 1], ag_ss.at[2], ag_rs.at[2], 1),
        dp_copy(w.at[0, 0], w.at[1, 0], ag_ss.at[3], ag_rs.at[3], 3),
        dp_copy(w.at[3, 0], w.at[2, 0], ag_ss.at[4], ag_rs.at[4], 1),
        dp_copy(w.at[1, 1], w.at[2, 1], ag_ss.at[5], ag_rs.at[5], 3),
    ]
    for copy in gather[:4]:
        copy.start()

    pack(1)
    pl.semaphore_wait(ready, GROUP - 1)

    @pl.loop(1, GROUP)
    def _(i):
        for d in (4, 3, 5, 2, 6, 1, 7, 0):
            row_copy(i, d).start()

        @pl.when(i < GROUP - 1)
        def _():
            pack(i + 1)

    g[...] = jnp.zeros_like(g)
    tacc[...] = jnp.zeros_like(tacc)

    def flip(k, m):
        wt_t[k, m] = jnp.transpose(w[k, m])

    gather[0].wait_recv()
    gather[4].start()
    gather[1].wait_recv()
    gather[5].start()
    flip(0, 0)
    flip(0, 1)
    flip(3, 0)
    flip(1, 1)
    gather[2].wait_recv()
    flip(3, 1)
    gather[3].wait_recv()
    flip(1, 0)
    gather[4].wait_recv()
    flip(2, 0)
    gather[5].wait_recv()
    flip(2, 1)

    reduce = [
        dp_copy(
            rs_s.at[n, pl.ds(128 * h, 128)], rs_r.at[n, pl.ds(128 * h, 128)],
            r_ss.at[n, h], r_rs.at[n, h], 1 if n in (0, 2, 4) else 3,
        )
        for n in range(6) for h in range(2)
    ]

    def reduce_start(n, h):
        reduce[2 * n + h].start()

    def reduce_wait(n):
        reduce[2 * n].wait_recv()
        reduce[2 * n + 1].wait_recv()
    others = pl.ds(1, GROUP - 1)
    rest = pl.ds(CAP, CHUNK - CAP)

    @pl.loop(0, GROUP)
    def _(t):
        @pl.when(t == 0)
        def _():
            plane_copy(send.at[0, rest], recv.at[0, rest], a_ss.at[0], a_rs.at[0], me).wait_recv()

        @pl.when(t != 0)
        def _():
            plane_copy(send.at[t], recv.at[t], a_ss.at[t], a_rs.at[t], me).wait_recv()

        feats = recv[t, :, :D]
        feats_f = feats.astype(f32)
        trunk_pre = dot(feats, wt[...])
        trunk_sig = sigmoid(trunk_pre)
        trunk_f = feats_f + trunk_pre * trunk_sig
        trunk_out = trunk_f.astype(bf16)
        trunk_t = jnp.transpose(trunk_f).astype(bf16)
        predicted = jnp.zeros((CHUNK, D), f32)
        for k in range(NX):
            up = dot(trunk_out, w[k, 0])
            sig = sigmoid(up)
            hid = up * sig
            hid_b = hid.astype(bf16)
            hbuf[k] = hid_b
            sbuf[k] = sig + hid * (1.0 - sig)
            predicted = predicted + dot(hid_b, wt_t[k, 1])
        errors = predicted - recv[t, :, D:].astype(f32)
        squares = errors * errors
        squares = jnp.transpose(squares[:, :128] + squares[:, 128:])
        lsend[t] = jnp.sum(squares, axis=0, keepdims=True) * (0.5 * loss_scale)

        @pl.when(t != 0)
        def _():
            plane_copy(
                lsend.at[t], lmid.at[t], s_ss.at[0], s_rs.at[0], before_in_group(t)
            ).start()

        scaled_f = errors * loss_scale
        scaled = scaled_f.astype(bf16)
        scaled_t = jnp.transpose(scaled_f).astype(bf16)
        row_grad = jnp.zeros((CHUNK, D), f32)
        for k in range(NX):
            pre_grad = (dot(scaled, w[k, 1]) * sbuf[k]).astype(bf16)
            pbuf[k] = pre_grad
            row_grad = row_grad + dot(pre_grad, wt_t[k, 0])
        slope = trunk_sig + trunk_pre * trunk_sig * (1.0 - trunk_sig)
        trunk_slope = (row_grad.astype(bf16).astype(f32) * slope).astype(bf16)
        tacc[...] += dot(jnp.transpose(feats_f).astype(bf16), trunk_slope)

        @pl.when(t == GROUP - 1)
        def _():
            for i in range(1, GROUP):
                to = in_group(i)
                share = pl.ds(pl.multiple_of((to % GROUP) * 32, 32), 32)
                plane_copy(tacc.at[share], tr.at[i], s_ss.at[1], s_rs.at[1], to).start()

        for k in (2, 1, 3, 0):
            g[k, 0] += dot(trunk_t, pbuf[k])
            g[k, 1] += dot(scaled_t, hbuf[k])
            if k:

                @pl.when(t == GROUP - 1)
                def _():
                    for n, m in {2: ((0, 0), (1, 1)), 1: ((2, 1),), 3: ((3, 0),)}[k]:
                        rs_s[n] = g[k, m].astype(bf16)
                    if k == 2:
                        for n, h in ((0, 0), (1, 0), (0, 1), (1, 1)):
                            reduce_start(n, h)

    tr[0] = tacc[pl.ds(pl.multiple_of(mg * 32, 32), 32)]
    lmid[0] = lsend[0]
    plane_copy(tr.at[others], tr.at[others], s_ss.at[1], s_rs.at[1], me).wait_recv()
    total = jnp.sum(tr[...], axis=0)
    for p in range(NZ):
        tz[p] = total[8 * (p % 4) : 8 * (p % 4) + 8, 128 * (p // 4) : 128 * (p // 4) + 128]
    for d in (4, 3, 5, 2, 6, 1, 7):
        plane_copy(tz.at[(mz + d) % NZ], zr.at[d], s_ss.at[2], s_rs.at[2], along_z(d)).start()
    zr[0] = tz[mz]
    reduce_start(2, 0)
    reduce_start(3, 0)

    plane_copy(lmid.at[others], lmid.at[others], s_ss.at[0], s_rs.at[0], me).wait_recv()
    for d in (4, 3, 5, 2, 6, 1, 7):
        plane_copy(lmid, lrecv.at[d], s_ss.at[3], s_rs.at[3], along_z(NZ - d)).start()
    lrecv[0] = lmid[...]

    reduce_wait(0)
    rs_s[4] = (g[1, 0] + rs_r[0].astype(f32)).astype(bf16)
    reduce_wait(1)
    rs_s[5] = (g[3, 1] + rs_r[1].astype(f32)).astype(bf16)

    plane_copy(zr.at[others], zr.at[others], s_ss.at[2], s_rs.at[2], me).wait_recv()
    xr[mx] = jnp.sum(zr[...], axis=0)
    for shift in (1, 2, 3):
        dp_copy(xr.at[mx], xr.at[mx], s_ss.at[4], s_rs.at[4], shift).start()

    for n, h in ((2, 1), (3, 1), (4, 0), (5, 0)):
        reduce_start(n, h)

    three = pl.ds(0, NX - 1)
    dp_copy(xr.at[three], xr.at[three], s_ss.at[4], s_rs.at[4], 1).wait_recv()
    agz[mz] = (xr[0] + xr[1]) + (xr[2] + xr[3])
    for d in (4, 3, 5, 2, 6, 1, 7):
        plane_copy(agz.at[mz], agz.at[mz], s_ss.at[5], s_rs.at[5], along_z(d)).start()
    reduce_start(4, 1)
    reduce_start(5, 1)

    plane_copy(lrecv.at[others], lrecv.at[others], s_ss.at[3], s_rs.at[3], me).wait_recv()
    table_f = lrecv[...].reshape(PLANE, CHUNK)
    high = table_f.astype(bf16)
    left = table_f - high.astype(f32)
    middle = left.astype(bf16)
    low = (left - middle.astype(f32)).astype(bf16)
    spot = place[...] & (CHUNK - 1)
    turned = (qrow[...] & (NZ - 1)) * GROUP + (qrow[...] >> 3)
    hot = onehot(lax.broadcasted_iota(i32, (PLANE, ROWS), 0) == turned)
    seen = sum(
        lax.dot_general(part, hot, (((0,), (0,)), ((), ())), preferred_element_type=f32)
        for part in (high, middle, low)
    )
    loss_out[...] = jnp.sum(
        jnp.where(lax.broadcasted_iota(i32, (CHUNK, ROWS), 0) == spot, seen, 0.0),
        axis=0,
        keepdims=True,
    )

    plane_copy(agz.at[others], agz.at[others], s_ss.at[5], s_rs.at[5], me).wait_recv()
    for i in range(1, GROUP):
        plane_copy(agz, agb.at[mg], s_ss.at[6], s_rs.at[6], in_group(i)).start()
    agb[mg] = agz[...]

    reduce_wait(2)
    reduce_wait(3)
    reduce_wait(4)
    gout[0] = g[0, 0] + rs_r[3].astype(f32) + rs_r[4].astype(f32)
    reduce_wait(5)
    gout[1] = g[0, 1] + rs_r[2].astype(f32) + rs_r[5].astype(f32)

    plane_copy(agb.at[others], agb.at[others], s_ss.at[6], s_rs.at[6], me).wait_recv()
    for i in range(GROUP):
        for p in range(NZ):
            row, col = 32 * i + 8 * (p % 4), 128 * (p // 4)
            tg_out[row : row + 8, col : col + 128] = agb[i, p]

    plane_copy(send.at[0, rest], recv.at[0, rest], a_ss.at[0], a_rs.at[0], me).wait_send()
    for i in range(1, GROUP):
        plane_copy(send.at[i], recv.at[i], a_ss.at[i], a_rs.at[i], me).wait_send()
    for copy in gather + reduce:
        copy.wait_send()
    for n, ref in ((0, lmid), (1, tr), (2, zr), (3, lrecv), (5, agz), (6, agb)):
        plane_copy(ref.at[others], ref.at[others], s_ss.at[n], s_rs.at[n], me).wait_send()
    dp_copy(xr.at[three], xr.at[three], s_ss.at[4], s_rs.at[4], 1).wait_send()


def on_device(
    cell_table, sample_index, region, targets, trunk_weight, expert_params, first_moment, second_moment
):
    vmem = pl.BlockSpec(memory_space=pltpu.VMEM)
    dma = pltpu.SemaphoreType.DMA
    grads, losses, trunk_grad = pl.pallas_call(
        fused,
        out_shape=(
            jax.ShapeDtypeStruct((2, D, SHARE), f32),
            jax.ShapeDtypeStruct((1, ROWS), f32),
            jax.ShapeDtypeStruct((D, D), f32),
        ),
        in_specs=[vmem] * 6,
        out_specs=(vmem, vmem, vmem),
        scratch_shapes=[
            pltpu.VMEM((GROUP, CHUNK, 2 * D), bf16),
            pltpu.VMEM((GROUP, CHUNK, 2 * D), bf16),
            pltpu.VMEM((NX, 2, D, SHARE), bf16),
            pltpu.VMEM((NX, 2, SHARE, D), bf16),
            pltpu.VMEM((NX, 2, D, SHARE), f32),
            pltpu.VMEM((ROWS, 2 * D), bf16),
            pltpu.VMEM((1, ROWS), i32),
            pltpu.VMEM((1, ROWS), i32),
            pltpu.VMEM((NX, CHUNK, SHARE), bf16),
            pltpu.VMEM((NX, CHUNK, SHARE), f32),
            pltpu.VMEM((NX, CHUNK, SHARE), bf16),
            pltpu.VMEM((D, D), f32),
            pltpu.VMEM((6, D, SHARE), bf16),
            pltpu.VMEM((6, D, SHARE), bf16),
            pltpu.VMEM((GROUP, 32, D), f32),
            pltpu.VMEM((NZ, 8, 128), f32),
            pltpu.VMEM((NZ, 8, 128), f32),
            pltpu.VMEM((NX, 8, 128), f32),
            pltpu.VMEM((NZ, 8, 128), f32),
            pltpu.VMEM((GROUP, NZ, 8, 128), f32),
            pltpu.VMEM((NZ, 1, CHUNK), f32),
            pltpu.VMEM((NZ, 1, CHUNK), f32),
            pltpu.VMEM((GROUP, NZ, 1, CHUNK), f32),
            dma((GROUP,)), dma((GROUP,)), pltpu.SemaphoreType.REGULAR,
            dma((6,)), dma((6,)),
            dma((6, 2)), dma((6, 2)),
            dma((7,)), dma((7,)),
        ],
        compiler_params=pltpu.CompilerParams(
            collective_id=0, has_side_effects=True, vmem_limit_bytes=56 << 20
        ),
        name="fused_step",
    )(
        cell_table,
        sample_index.reshape(1, ROWS),
        region.reshape(1, ROWS),
        targets,
        trunk_weight,
        expert_params[0],
    )
    new_params, new_first, new_second = adam_update(
        expert_params, first_moment, second_moment, grads[None]
    )
    return (trunk_grad, losses.reshape(ROWS), new_params, new_first, new_second)


def solution(mesh):
    placed = (
        P(("dp", "expert"), None),
        P(("dp", "expert")),
        P(("dp", "expert"), None),
        P(("dp", "expert"), None),
        P(),
        P("expert", None, None, "dp"),
        P("expert", None, None, "dp"),
        P("expert", None, None, "dp"),
    )
    return jax.shard_map(
        on_device,
        mesh=mesh,
        in_specs=placed,
        out_specs=(
            P(),
            P(("dp", "expert")),
            P("expert", None, None, "dp"),
            P("expert", None, None, "dp"),
            P("expert", None, None, "dp"),
        ),
        check_vma=False,
    )
```

```python
import jax
import jax.numpy as jnp
from jax import lax
from jax.experimental import pallas as pl
from jax.experimental.pallas import tpu as pltpu
from jax.sharding import PartitionSpec as P

MESH = pl.DeviceIdType.MESH
bf16 = jnp.bfloat16
f32 = jnp.float32
i32 = jnp.int32

loss_scale = 1.0 / 32.0
beta_one = 0.9
beta_two = 0.999
learn_rate = 0.05
adam_eps = 1e-08
adam_step = 10

NZ, NY, NC, NX = 8, 4, 2, 4
PLANE = NZ * NY * NC
GROUP = NY * NC
D = 256
ROWS = 1024
CELLS = 2048
CAP = 32
CHUNK = GROUP * CAP
SHARE = 512
HALF = CHUNK
POS = (3, 6, 4, 1, 0, 2, 5, 7)
FAR = (4, 3, 5, 0, 2, 6, 1, 7)


def order_of(t):
    return t


def adam_update(params, first, second, grads):
    first_new = beta_one * first + (1.0 - beta_one) * grads
    second_new = beta_two * second + (1.0 - beta_two) * grads * grads
    first_hat = first_new / (1.0 - beta_one**adam_step)
    second_hat = second_new / (1.0 - beta_two**adam_step)
    return (
        params - learn_rate * first_hat / (jnp.sqrt(second_hat) + adam_eps),
        first_new,
        second_new,
    )


def dot(a, b):
    return jnp.dot(a, b, preferred_element_type=f32)


def sigmoid(v):
    return 0.5 + 0.5 * jnp.tanh(0.5 * v)


def onehot(mask):
    return jnp.where(mask, 1.0, 0.0).astype(bf16)


def fused(
    table_in, sidx_in, region_in, targets_in, wt_in, params_in,
    gout, loss_out, tg_out,
    table, params, sidx, region, wt, in_sem, send, recv, w, wt_t, g, pay, qrow, place, hbuf, sbuf, pbuf, tacc,
    rs_s, rs_r, tr, tz, zr, xr, agz, agb, lsend, lmid, lrecv,
    a_ss, a_rs, ready, ag_ss, ag_rs, r_ss, r_rs, s_ss, s_rs,
):
    me = lax.axis_index("expert")
    mx = lax.axis_index("dp")
    mz = me // GROUP
    my = (me // NC) % NY
    mc = me % NC
    mg = me % GROUP

    def along_z(d):
        return ((mz + d) % NZ) * GROUP + mg

    def in_group(i):
        return mz * GROUP + ((my + i // NC) % NY) * NC + (mc + i % NC) % NC

    def before_in_group(i):
        return mz * GROUP + ((my + NY - i // NC) % NY) * NC + (mc + NC - i % NC) % NC

    def owner(i, d):
        return ((mz + d) % NZ) * GROUP + ((my + i // NC) % NY) * NC + (mc + i % NC) % NC

    def plane_copy(src, dst, ss, rs, to):
        return pltpu.make_async_remote_copy(
            src_ref=src, dst_ref=dst, send_sem=ss, recv_sem=rs,
            device_id={"expert": to}, device_id_type=MESH,
        )

    def dp_copy(src, dst, ss, rs, shift):
        return pltpu.make_async_remote_copy(
            src_ref=src, dst_ref=dst, send_sem=ss, recv_sem=rs,
            device_id={"dp": (mx + shift) % NX}, device_id_type=MESH,
        )

    loads = [
        pltpu.make_async_copy(params_in, params, in_sem.at[0]),
        pltpu.make_async_copy(table_in, table, in_sem.at[1]),
        pltpu.make_async_copy(targets_in, pay.at[:, pl.ds(D, D)], in_sem.at[2]),
        pltpu.make_async_copy(region_in, region, in_sem.at[3]),
        pltpu.make_async_copy(sidx_in, sidx, in_sem.at[4]),
        pltpu.make_async_copy(wt_in, wt, in_sem.at[5]),
    ]
    for n in (3, 4, 1, 2, 0, 5):
        loads[n].start()

    barrier = pltpu.get_barrier_semaphore()
    for d in (4, 3, 5, 2, 6, 1, 7):
        pl.semaphore_signal(barrier, inc=1, device_id={"expert": along_z(d)}, device_id_type=MESH)
    for i in range(1, GROUP):
        pl.semaphore_signal(barrier, inc=1, device_id={"expert": in_group(i)}, device_id_type=MESH)
    for shift in (1, 2, 3):
        pl.semaphore_signal(
            barrier, inc=1, device_id={"dp": (mx + shift) % NX}, device_id_type=MESH
        )

    loads[3].wait()
    named = region[...]
    q = (
        ((((named >> 1) & (NY - 1)) - my) & (NY - 1)) * NC * NZ
        + (((named & 1) - mc) & (NC - 1)) * NZ
        + (((named >> 3) - mz) & (NZ - 1))
    )
    qrow[...] = q
    along = q & (NZ - 1)
    spread = q - along + sum(jnp.where(along == d, POS[d], 0) for d in range(NZ))
    before = onehot(
        lax.broadcasted_iota(i32, (256, 256), 0) < lax.broadcasted_iota(i32, (256, 256), 1)
    )
    carry = jnp.zeros((PLANE, 1), f32)
    for b in range(ROWS // 256):
        part = q[:, 256 * b : 256 * b + 256]
        hot = jnp.where(lax.broadcasted_iota(i32, (PLANE, 256), 0) == part, 1.0, 0.0)
        count = dot(hot.astype(bf16), before) + carry
        slot = jnp.sum(hot * count, axis=0, keepdims=True)
        carry = carry + jnp.sum(hot, axis=1, keepdims=True)
        place[:, 256 * b : 256 * b + 256] = spread[:, 256 * b : 256 * b + 256] * CAP + slot.astype(i32)

    loads[1].wait()
    loads[4].wait()
    for b in range(ROWS // 256):
        cols = [
            jnp.transpose(
                jnp.broadcast_to(
                    sidx[:, 256 * b + 128 * h : 256 * b + 128 * h + 128].astype(f32), (128, 128)
                )
            )
            for h in range(2)
        ]
        col = jnp.concatenate(cols, axis=0).astype(i32)
        wide = jnp.concatenate([col] * (CELLS // 128), axis=1)
        pick = onehot(wide == lax.broadcasted_iota(i32, (256, CELLS), 1))
        pay[256 * b : 256 * b + 256, :D] = dot(pick, table[...]).astype(bf16)
    loads[2].wait()

    def pack(i):
        mask = lax.broadcasted_iota(i32, (CHUNK, ROWS), 0) + i * CHUNK == place[...]
        send[i] = dot(onehot(mask), pay[...]).astype(bf16)

    def row_copy(i, d):
        rows = pl.ds(POS[d] * CAP, CAP)
        h = POS[d] * CAP // HALF
        return plane_copy(
            send.at[i, rows], recv.at[i, rows], a_ss.at[i, h], a_rs.at[i, h], owner(i, d)
        )

    pack(0)
    own = POS[0] * CAP
    recv[0, own : own + CAP] = send[0, own : own + CAP]
    loads[0].wait()
    loads[5].wait()
    w[0] = params[...].astype(bf16)
    pl.semaphore_wait(barrier, NZ - 1 + GROUP - 1 + NX - 1)
    for d in FAR:
        if d:
            row_copy(0, d).start()

    for i in range(1, GROUP):
        pl.semaphore_signal(ready, inc=1, device_id={"expert": in_group(i)}, device_id_type=MESH)

    gather = [
        dp_copy(w.at[0, 0], w.at[3, 0], ag_ss.at[0], ag_rs.at[0], 1),
        dp_copy(w.at[0, 1], w.at[1, 1], ag_ss.at[1], ag_rs.at[1], 3),
        dp_copy(w.at[0, 1], w.at[3, 1], ag_ss.at[2], ag_rs.at[2], 1),
        dp_copy(w.at[0, 0], w.at[1, 0], ag_ss.at[3], ag_rs.at[3], 3),
        dp_copy(w.at[3, 0], w.at[2, 0], ag_ss.at[4], ag_rs.at[4], 1),
        dp_copy(w.at[1, 1], w.at[2, 1], ag_ss.at[5], ag_rs.at[5], 3),
    ]
    for copy in gather[:4]:
        copy.start()

    pack(order_of(1))
    pl.semaphore_wait(ready, GROUP - 1)

    @pl.loop(1, GROUP)
    def _(t):
        for d in FAR:
            row_copy(order_of(t), d).start()

        @pl.when(t < GROUP - 1)
        def _():
            pack(order_of(t + 1))

    g[...] = jnp.zeros_like(g)
    tacc[...] = jnp.zeros_like(tacc)

    def flip(k, m):
        wt_t[k, m] = jnp.transpose(w[k, m])

    gather[0].wait_recv()
    gather[4].start()
    gather[1].wait_recv()
    gather[5].start()
    flip(0, 0)
    flip(0, 1)
    flip(3, 0)
    flip(1, 1)
    gather[2].wait_recv()
    flip(3, 1)
    gather[3].wait_recv()
    flip(1, 0)
    gather[4].wait_recv()
    flip(2, 0)
    gather[5].wait_recv()
    flip(2, 1)

    reduce = [
        dp_copy(
            rs_s.at[n, pl.ds(128 * h, 128)], rs_r.at[n, pl.ds(128 * h, 128)],
            r_ss.at[n, h], r_rs.at[n, h], 1 if n in (0, 2, 4) else 3,
        )
        for n in range(6) for h in range(2)
    ]

    def reduce_start(n, h):
        reduce[2 * n + h].start()

    def reduce_wait(n):
        reduce[2 * n].wait_recv()
        reduce[2 * n + 1].wait_recv()
    others = pl.ds(1, GROUP - 1)

    def half(ref_a, ref_b, i, h, first):
        rows = pl.ds(h * HALF if isinstance(h, int) else pl.multiple_of(h * HALF, HALF), HALF - CAP if first else HALF)
        return plane_copy(ref_a.at[i, rows], ref_b.at[i, rows], a_ss.at[i, h], a_rs.at[i, h], me)

    @pl.loop(0, GROUP)
    def _(t):
        i = order_of(t)
        h = 0

        @pl.when(t == 0)
        def _():
            half(send, recv, 0, 0, True).wait_recv()

        @pl.when(t != 0)
        def _():
            half(send, recv, i, h, False).wait_recv()

        rows = pl.ds(pl.multiple_of(h * HALF, HALF), HALF)
        feats = recv[i, rows, :D]
        feats_f = feats.astype(f32)
        trunk_pre = dot(feats, wt[...])
        trunk_sig = sigmoid(trunk_pre)
        trunk_f = feats_f + trunk_pre * trunk_sig
        trunk_out = trunk_f.astype(bf16)
        trunk_t = jnp.transpose(trunk_f).astype(bf16)
        predicted = jnp.zeros((HALF, D), f32)
        for k in range(NX):
            up = dot(trunk_out, w[k, 0])
            sig = sigmoid(up)
            hid = up * sig
            hid_b = hid.astype(bf16)
            hbuf[k] = hid_b
            sbuf[k] = sig + hid * (1.0 - sig)
            predicted = predicted + dot(hid_b, wt_t[k, 1])
        errors = predicted - recv[i, rows, D:].astype(f32)
        squares = errors * errors
        squares = jnp.transpose(squares[:, :128] + squares[:, 128:])
        lsend[i, h] = jnp.sum(squares, axis=0, keepdims=True) * (0.5 * loss_scale)

        @pl.when(i != 0)
        def _():
            plane_copy(
                lsend.at[i], lmid.at[i], s_ss.at[0], s_rs.at[0], before_in_group(i)
            ).start()

        scaled_f = errors * loss_scale
        scaled = scaled_f.astype(bf16)
        scaled_t = jnp.transpose(scaled_f).astype(bf16)
        row_grad = jnp.zeros((HALF, D), f32)
        for k in range(NX):
            pre_grad = (dot(scaled, w[k, 1]) * sbuf[k]).astype(bf16)
            pbuf[k] = pre_grad
            row_grad = row_grad + dot(pre_grad, wt_t[k, 0])
        slope = trunk_sig + trunk_pre * trunk_sig * (1.0 - trunk_sig)
        trunk_slope = (row_grad.astype(bf16).astype(f32) * slope).astype(bf16)
        tacc[...] += dot(jnp.transpose(feats_f).astype(bf16), trunk_slope)

        @pl.when(t == GROUP - 1)
        def _():
            for i in range(1, GROUP):
                to = in_group(i)
                share = pl.ds(pl.multiple_of((to % GROUP) * 32, 32), 32)
                plane_copy(tacc.at[share], tr.at[i], s_ss.at[1], s_rs.at[1], to).start()

        for k in (2, 1, 3, 0):
            g[k, 0] += dot(trunk_t, pbuf[k])
            g[k, 1] += dot(scaled_t, hbuf[k])
            if k:

                @pl.when(t == GROUP - 1)
                def _():
                    for n, m in {2: ((0, 0), (1, 1)), 1: ((2, 1),), 3: ((3, 0),)}[k]:
                        rs_s[n] = g[k, m].astype(bf16)
                    if k == 2:
                        for n, h in ((0, 0), (1, 0), (0, 1), (1, 1)):
                            reduce_start(n, h)

    tr[0] = tacc[pl.ds(pl.multiple_of(mg * 32, 32), 32)]
    lmid[0] = lsend[0]
    plane_copy(tr.at[others], tr.at[others], s_ss.at[1], s_rs.at[1], me).wait_recv()
    total = jnp.sum(tr[...], axis=0)
    for p in range(NZ):
        tz[p] = total[8 * (p % 4) : 8 * (p % 4) + 8, 128 * (p // 4) : 128 * (p // 4) + 128]
    for d in (4, 3, 5, 2, 6, 1, 7):
        plane_copy(tz.at[(mz + d) % NZ], zr.at[d], s_ss.at[2], s_rs.at[2], along_z(d)).start()
    zr[0] = tz[mz]
    reduce_start(2, 0)
    reduce_start(3, 0)

    plane_copy(lmid.at[others], lmid.at[others], s_ss.at[0], s_rs.at[0], me).wait_recv()
    for d in (4, 3, 5, 2, 6, 1, 7):
        plane_copy(lmid, lrecv.at[d], s_ss.at[3], s_rs.at[3], along_z(NZ - d)).start()
    lrecv[0] = lmid[...]

    reduce_wait(0)
    rs_s[4] = (g[1, 0] + rs_r[0].astype(f32)).astype(bf16)
    reduce_wait(1)
    rs_s[5] = (g[3, 1] + rs_r[1].astype(f32)).astype(bf16)

    plane_copy(zr.at[others], zr.at[others], s_ss.at[2], s_rs.at[2], me).wait_recv()
    xr[mx] = jnp.sum(zr[...], axis=0)
    for shift in (1, 2, 3):
        dp_copy(xr.at[mx], xr.at[mx], s_ss.at[4], s_rs.at[4], shift).start()

    for n, h in ((2, 1), (3, 1), (4, 0), (5, 0)):
        reduce_start(n, h)

    three = pl.ds(0, NX - 1)
    dp_copy(xr.at[three], xr.at[three], s_ss.at[4], s_rs.at[4], 1).wait_recv()
    agz[mz] = (xr[0] + xr[1]) + (xr[2] + xr[3])
    for d in (4, 3, 5, 2, 6, 1, 7):
        plane_copy(agz.at[mz], agz.at[mz], s_ss.at[5], s_rs.at[5], along_z(d)).start()
    reduce_start(4, 1)
    reduce_start(5, 1)

    plane_copy(lrecv.at[others], lrecv.at[others], s_ss.at[3], s_rs.at[3], me).wait_recv()
    table_f = jnp.concatenate(
        [lrecv[:, :, h].reshape(PLANE, HALF) for h in range(CHUNK // HALF)], axis=1
    )
    high = table_f.astype(bf16)
    left = table_f - high.astype(f32)
    middle = left.astype(bf16)
    low = (left - middle.astype(f32)).astype(bf16)
    spot = place[...] & (CHUNK - 1)
    turned = (qrow[...] & (NZ - 1)) * GROUP + (qrow[...] >> 3)
    hot = onehot(lax.broadcasted_iota(i32, (PLANE, ROWS), 0) == turned)
    seen = sum(
        lax.dot_general(part, hot, (((0,), (0,)), ((), ())), preferred_element_type=f32)
        for part in (high, middle, low)
    )
    loss_out[...] = jnp.sum(
        jnp.where(lax.broadcasted_iota(i32, (CHUNK, ROWS), 0) == spot, seen, 0.0),
        axis=0,
        keepdims=True,
    )

    plane_copy(agz.at[others], agz.at[others], s_ss.at[5], s_rs.at[5], me).wait_recv()
    for i in range(1, GROUP):
        plane_copy(agz, agb.at[mg], s_ss.at[6], s_rs.at[6], in_group(i)).start()
    agb[mg] = agz[...]

    reduce_wait(2)
    reduce_wait(3)
    reduce_wait(4)
    gout[0] = g[0, 0] + rs_r[3].astype(f32) + rs_r[4].astype(f32)
    reduce_wait(5)
    gout[1] = g[0, 1] + rs_r[2].astype(f32) + rs_r[5].astype(f32)

    plane_copy(agb.at[others], agb.at[others], s_ss.at[6], s_rs.at[6], me).wait_recv()
    for i in range(GROUP):
        for p in range(NZ):
            row, col = 32 * i + 8 * (p % 4), 128 * (p // 4)
            tg_out[row : row + 8, col : col + 128] = agb[i, p]

    for i in range(GROUP):
        for h in range(CHUNK // HALF):
            half(send, recv, i, h, i == 0 and h == 0).wait_send()
    for copy in gather + reduce:
        copy.wait_send()
    for n, ref in ((0, lmid), (1, tr), (2, zr), (3, lrecv), (5, agz), (6, agb)):
        plane_copy(ref.at[others], ref.at[others], s_ss.at[n], s_rs.at[n], me).wait_send()
    dp_copy(xr.at[three], xr.at[three], s_ss.at[4], s_rs.at[4], 1).wait_send()


def on_device(
    cell_table, sample_index, region, targets, trunk_weight, expert_params, first_moment, second_moment
):
    vmem = pl.BlockSpec(memory_space=pltpu.VMEM)
    hbm = pl.BlockSpec(memory_space=pltpu.HBM)
    dma = pltpu.SemaphoreType.DMA
    grads, losses, trunk_grad = pl.pallas_call(
        fused,
        out_shape=(
            jax.ShapeDtypeStruct((2, D, SHARE), f32),
            jax.ShapeDtypeStruct((1, ROWS), f32),
            jax.ShapeDtypeStruct((D, D), f32),
        ),
        in_specs=[hbm] * 6,
        out_specs=(vmem, vmem, vmem),
        scratch_shapes=[
            pltpu.VMEM((CELLS, D), bf16),
            pltpu.VMEM((2, D, SHARE), f32),
            pltpu.VMEM((1, ROWS), i32),
            pltpu.VMEM((1, ROWS), i32),
            pltpu.VMEM((D, D), bf16),
            dma((6,)),
            pltpu.VMEM((GROUP, CHUNK, 2 * D), bf16),
            pltpu.VMEM((GROUP, CHUNK, 2 * D), bf16),
            pltpu.VMEM((NX, 2, D, SHARE), bf16),
            pltpu.VMEM((NX, 2, SHARE, D), bf16),
            pltpu.VMEM((NX, 2, D, SHARE), f32),
            pltpu.VMEM((ROWS, 2 * D), bf16),
            pltpu.VMEM((1, ROWS), i32),
            pltpu.VMEM((1, ROWS), i32),
            pltpu.VMEM((NX, HALF, SHARE), bf16),
            pltpu.VMEM((NX, HALF, SHARE), f32),
            pltpu.VMEM((NX, HALF, SHARE), bf16),
            pltpu.VMEM((D, D), f32),
            pltpu.VMEM((6, D, SHARE), bf16),
            pltpu.VMEM((6, D, SHARE), bf16),
            pltpu.VMEM((GROUP, 32, D), f32),
            pltpu.VMEM((NZ, 8, 128), f32),
            pltpu.VMEM((NZ, 8, 128), f32),
            pltpu.VMEM((NX, 8, 128), f32),
            pltpu.VMEM((NZ, 8, 128), f32),
            pltpu.VMEM((GROUP, NZ, 8, 128), f32),
            pltpu.VMEM((GROUP, 1, 1, HALF), f32),
            pltpu.VMEM((GROUP, 1, 1, HALF), f32),
            pltpu.VMEM((NZ, GROUP, 1, 1, HALF), f32),
            dma((GROUP, 1)), dma((GROUP, 1)), pltpu.SemaphoreType.REGULAR,
            dma((6,)), dma((6,)),
            dma((6, 2)), dma((6, 2)),
            dma((7,)), dma((7,)),
        ],
        compiler_params=pltpu.CompilerParams(
            collective_id=0, has_side_effects=True, vmem_limit_bytes=36 << 20
        ),
        name="fused_step",
    )(
        *(
            pltpu.with_memory_space_constraint(value, pltpu.HBM)
            for value in (
                cell_table,
                sample_index.reshape(1, ROWS),
                region.reshape(1, ROWS),
                targets,
                trunk_weight,
                expert_params[0],
            )
        )
    )
    new_params, new_first, new_second = adam_update(
        expert_params, first_moment, second_moment, grads[None]
    )
    return (trunk_grad, losses.reshape(ROWS), new_params, new_first, new_second)


def solution(mesh):
    placed = (
        P(("dp", "expert"), None),
        P(("dp", "expert")),
        P(("dp", "expert"), None),
        P(("dp", "expert"), None),
        P(),
        P("expert", None, None, "dp"),
        P("expert", None, None, "dp"),
        P("expert", None, None, "dp"),
    )
    return jax.shard_map(
        on_device,
        mesh=mesh,
        in_specs=placed,
        out_specs=(
            P(),
            P(("dp", "expert")),
            P("expert", None, None, "dp"),
            P("expert", None, None, "dp"),
            P("expert", None, None, "dp"),
        ),
        check_vma=False,
    )
```

```python
import jax
import jax.numpy as jnp
from jax import lax
from jax.experimental import pallas as pl
from jax.experimental.pallas import tpu as pltpu
from jax.sharding import PartitionSpec as P

MESH = pl.DeviceIdType.MESH
bf16 = jnp.bfloat16
f32 = jnp.float32
i32 = jnp.int32

loss_scale = 1.0 / 32.0
beta_one = 0.9
beta_two = 0.999
learn_rate = 0.05
adam_eps = 1e-08
adam_step = 10

NZ, NY, NC, NX = 8, 4, 2, 4
PLANE = NZ * NY * NC
GROUP = NY * NC
D = 256
ROWS = 1024
CELLS = 2048
CAP = 32
CHUNK = GROUP * CAP
SHARE = 512
HALF = CHUNK
POS = (3, 6, 4, 1, 0, 2, 5, 7)
FAR = (4, 3, 5, 0, 2, 6, 1, 7)


def order_of(t):
    return t


def adam_update(params, first, second, grads):
    first_new = beta_one * first + (1.0 - beta_one) * grads
    second_new = beta_two * second + (1.0 - beta_two) * grads * grads
    root = jnp.sqrt(second_new * (1.0 / (1.0 - beta_two**adam_step)))
    step = first_new * (learn_rate / (1.0 - beta_one**adam_step))
    return (params - step / (root + adam_eps), first_new, second_new)


def dot(a, b):
    return jnp.dot(a, b, preferred_element_type=f32)


def sigmoid(v):
    return 0.5 + 0.5 * jnp.tanh(0.5 * v)


def onehot(mask):
    return jnp.where(mask, 1.0, 0.0).astype(bf16)


def fused(
    table_in, sidx_in, region_in, targets_in, wt_in, params_in,
    gout, loss_out, tg_out,
    table, params, sidx, region, wt, in_sem, send, recv, w, wt_t, g, pay, qrow, place, hbuf, sbuf, pbuf, tacc,
    rs_s, rs_r, tr, tz, zr, xr, agz, agb, lsend, lmid, lrecv,
    a_ss, a_rs, ready, ag_ss, ag_rs, r_ss, r_rs, s_ss, s_rs,
):
    me = lax.axis_index("expert")
    mx = lax.axis_index("dp")
    mz = me // GROUP
    my = (me // NC) % NY
    mc = me % NC
    mg = me % GROUP

    def along_z(d):
        return ((mz + d) % NZ) * GROUP + mg

    def in_group(i):
        return mz * GROUP + ((my + i // NC) % NY) * NC + (mc + i % NC) % NC

    def before_in_group(i):
        return mz * GROUP + ((my + NY - i // NC) % NY) * NC + (mc + NC - i % NC) % NC

    def owner(i, d):
        return ((mz + d) % NZ) * GROUP + ((my + i // NC) % NY) * NC + (mc + i % NC) % NC

    def plane_copy(src, dst, ss, rs, to):
        return pltpu.make_async_remote_copy(
            src_ref=src, dst_ref=dst, send_sem=ss, recv_sem=rs,
            device_id={"expert": to}, device_id_type=MESH,
        )

    def dp_copy(src, dst, ss, rs, shift):
        return pltpu.make_async_remote_copy(
            src_ref=src, dst_ref=dst, send_sem=ss, recv_sem=rs,
            device_id={"dp": (mx + shift) % NX}, device_id_type=MESH,
        )

    loads = [
        pltpu.make_async_copy(params_in, params, in_sem.at[0]),
        pltpu.make_async_copy(table_in, table, in_sem.at[1]),
        pltpu.make_async_copy(targets_in, pay.at[:, pl.ds(D, D)], in_sem.at[2]),
        pltpu.make_async_copy(region_in, region, in_sem.at[3]),
        pltpu.make_async_copy(sidx_in, sidx, in_sem.at[4]),
        pltpu.make_async_copy(wt_in, wt, in_sem.at[5]),
    ]
    for n in (3, 4, 1, 2, 0, 5):
        loads[n].start()

    barrier = pltpu.get_barrier_semaphore()
    for d in (4, 3, 5, 2, 6, 1, 7):
        pl.semaphore_signal(barrier, inc=1, device_id={"expert": along_z(d)}, device_id_type=MESH)
    for i in range(1, GROUP):
        pl.semaphore_signal(barrier, inc=1, device_id={"expert": in_group(i)}, device_id_type=MESH)
    for shift in (1, 2, 3):
        pl.semaphore_signal(
            barrier, inc=1, device_id={"dp": (mx + shift) % NX}, device_id_type=MESH
        )

    loads[3].wait()
    named = region[...]
    q = (
        ((((named >> 1) & (NY - 1)) - my) & (NY - 1)) * NC * NZ
        + (((named & 1) - mc) & (NC - 1)) * NZ
        + (((named >> 3) - mz) & (NZ - 1))
    )
    qrow[...] = q
    along = q & (NZ - 1)
    spread = q - along + sum(jnp.where(along == d, POS[d], 0) for d in range(NZ))
    before = onehot(
        lax.broadcasted_iota(i32, (256, 256), 0) < lax.broadcasted_iota(i32, (256, 256), 1)
    )
    carry = jnp.zeros((PLANE, 1), f32)
    for b in range(ROWS // 256):
        part = q[:, 256 * b : 256 * b + 256]
        hot = jnp.where(lax.broadcasted_iota(i32, (PLANE, 256), 0) == part, 1.0, 0.0)
        count = dot(hot.astype(bf16), before) + carry
        slot = jnp.sum(hot * count, axis=0, keepdims=True)
        carry = carry + jnp.sum(hot, axis=1, keepdims=True)
        place[:, 256 * b : 256 * b + 256] = spread[:, 256 * b : 256 * b + 256] * CAP + slot.astype(i32)

    loads[1].wait()
    loads[4].wait()
    for b in range(ROWS // 256):
        cols = [
            jnp.transpose(
                jnp.broadcast_to(
                    sidx[:, 256 * b + 128 * h : 256 * b + 128 * h + 128].astype(f32), (128, 128)
                )
            )
            for h in range(2)
        ]
        col = jnp.concatenate(cols, axis=0).astype(i32)
        wide = jnp.concatenate([col] * (CELLS // 128), axis=1)
        pick = onehot(wide == lax.broadcasted_iota(i32, (256, CELLS), 1))
        pay[256 * b : 256 * b + 256, :D] = dot(pick, table[...]).astype(bf16)
    loads[2].wait()

    def pack(i):
        mask = lax.broadcasted_iota(i32, (CHUNK, ROWS), 0) + i * CHUNK == place[...]
        send[i] = dot(onehot(mask), pay[...]).astype(bf16)

    def row_copy(i, d):
        rows = pl.ds(POS[d] * CAP, CAP)
        h = POS[d] * CAP // HALF
        return plane_copy(
            send.at[i, rows], recv.at[i, rows], a_ss.at[i, h], a_rs.at[i, h], owner(i, d)
        )

    pack(0)
    own = POS[0] * CAP
    recv[0, own : own + CAP] = send[0, own : own + CAP]
    loads[0].wait()
    loads[5].wait()
    w[0] = params[...].astype(bf16)
    pl.semaphore_wait(barrier, NZ - 1 + GROUP - 1 + NX - 1)
    for d in FAR:
        if d:
            row_copy(0, d).start()

    for i in range(1, GROUP):
        pl.semaphore_signal(ready, inc=1, device_id={"expert": in_group(i)}, device_id_type=MESH)

    gather = [
        dp_copy(w.at[0, 0], w.at[3, 0], ag_ss.at[0], ag_rs.at[0], 1),
        dp_copy(w.at[0, 1], w.at[1, 1], ag_ss.at[1], ag_rs.at[1], 3),
        dp_copy(w.at[0, 1], w.at[3, 1], ag_ss.at[2], ag_rs.at[2], 1),
        dp_copy(w.at[0, 0], w.at[1, 0], ag_ss.at[3], ag_rs.at[3], 3),
        dp_copy(w.at[3, 0], w.at[2, 0], ag_ss.at[4], ag_rs.at[4], 1),
        dp_copy(w.at[1, 1], w.at[2, 1], ag_ss.at[5], ag_rs.at[5], 3),
    ]
    for copy in gather[:4]:
        copy.start()

    pack(order_of(1))
    pl.semaphore_wait(ready, GROUP - 1)

    @pl.loop(1, GROUP)
    def _(t):
        for d in FAR:
            row_copy(order_of(t), d).start()

        @pl.when(t < GROUP - 1)
        def _():
            pack(order_of(t + 1))

    g[...] = jnp.zeros_like(g)
    tacc[...] = jnp.zeros_like(tacc)

    def flip(k, m):
        wt_t[k, m] = jnp.transpose(w[k, m])

    gather[0].wait_recv()
    gather[4].start()
    gather[1].wait_recv()
    gather[5].start()
    flip(0, 0)
    flip(0, 1)
    flip(3, 0)
    flip(1, 1)
    gather[2].wait_recv()
    flip(3, 1)
    gather[3].wait_recv()
    flip(1, 0)
    gather[4].wait_recv()
    flip(2, 0)
    gather[5].wait_recv()
    flip(2, 1)

    reduce = [
        dp_copy(
            rs_s.at[n, pl.ds(128 * h, 128)], rs_r.at[n, pl.ds(128 * h, 128)],
            r_ss.at[n, h], r_rs.at[n, h], 1 if n in (0, 2, 4) else 3,
        )
        for n in range(6) for h in range(2)
    ]

    def reduce_start(n, h):
        reduce[2 * n + h].start()

    def reduce_wait(n):
        reduce[2 * n].wait_recv()
        reduce[2 * n + 1].wait_recv()
    others = pl.ds(1, GROUP - 1)

    def half(ref_a, ref_b, i, h, first):
        rows = pl.ds(h * HALF if isinstance(h, int) else pl.multiple_of(h * HALF, HALF), HALF - CAP if first else HALF)
        return plane_copy(ref_a.at[i, rows], ref_b.at[i, rows], a_ss.at[i, h], a_rs.at[i, h], me)

    @pl.loop(0, GROUP)
    def _(t):
        i = order_of(t)
        h = 0

        @pl.when(t == 0)
        def _():
            half(send, recv, 0, 0, True).wait_recv()

        @pl.when(t != 0)
        def _():
            half(send, recv, i, h, False).wait_recv()

        rows = pl.ds(pl.multiple_of(h * HALF, HALF), HALF)
        feats = recv[i, rows, :D]
        feats_f = feats.astype(f32)
        trunk_pre = dot(feats, wt[...])
        trunk_sig = sigmoid(trunk_pre)
        trunk_f = feats_f + trunk_pre * trunk_sig
        trunk_out = trunk_f.astype(bf16)
        trunk_t = jnp.transpose(trunk_f).astype(bf16)
        predicted = jnp.zeros((HALF, D), f32)
        for k in range(NX):
            up = dot(trunk_out, w[k, 0])
            sig = sigmoid(up)
            hid = up * sig
            hid_b = hid.astype(bf16)
            hbuf[k] = hid_b
            sbuf[k] = sig + hid * (1.0 - sig)
            predicted = predicted + dot(hid_b, wt_t[k, 1])
        errors = predicted - recv[i, rows, D:].astype(f32)
        squares = errors * errors
        squares = jnp.transpose(squares[:, :128] + squares[:, 128:])
        lsend[i, h] = jnp.sum(squares, axis=0, keepdims=True) * (0.5 * loss_scale)

        @pl.when(i != 0)
        def _():
            plane_copy(
                lsend.at[i], lmid.at[i], s_ss.at[0], s_rs.at[0], before_in_group(i)
            ).start()

        scaled_f = errors * loss_scale
        scaled = scaled_f.astype(bf16)
        scaled_t = jnp.transpose(scaled_f).astype(bf16)
        row_grad = jnp.zeros((HALF, D), f32)
        for k in range(NX):
            pre_grad = (dot(scaled, w[k, 1]) * sbuf[k]).astype(bf16)
            pbuf[k] = pre_grad
            row_grad = row_grad + dot(pre_grad, wt_t[k, 0])
        slope = trunk_sig + trunk_pre * trunk_sig * (1.0 - trunk_sig)
        trunk_slope = (row_grad.astype(bf16).astype(f32) * slope).astype(bf16)
        tacc[...] += dot(jnp.transpose(feats_f).astype(bf16), trunk_slope)

        @pl.when(t == GROUP - 1)
        def _():
            for i in range(1, GROUP):
                to = in_group(i)
                share = pl.ds(pl.multiple_of((to % GROUP) * 32, 32), 32)
                plane_copy(tacc.at[share], tr.at[i], s_ss.at[1], s_rs.at[1], to).start()

        for k in (2, 1, 3, 0):
            g[k, 0] += dot(trunk_t, pbuf[k])
            g[k, 1] += dot(scaled_t, hbuf[k])
            if k:

                @pl.when(t == GROUP - 1)
                def _():
                    for n, m in {2: ((0, 0), (1, 1)), 1: ((2, 1),), 3: ((3, 0),)}[k]:
                        rs_s[n] = g[k, m].astype(bf16)
                    if k == 2:
                        for n, h in ((0, 0), (1, 0), (0, 1), (1, 1)):
                            reduce_start(n, h)

    tr[0] = tacc[pl.ds(pl.multiple_of(mg * 32, 32), 32)]
    lmid[0] = lsend[0]
    plane_copy(tr.at[others], tr.at[others], s_ss.at[1], s_rs.at[1], me).wait_recv()
    total = jnp.sum(tr[...], axis=0)
    for p in range(NZ):
        tz[p] = total[8 * (p % 4) : 8 * (p % 4) + 8, 128 * (p // 4) : 128 * (p // 4) + 128]
    for d in (4, 3, 5, 2, 6, 1, 7):
        plane_copy(tz.at[(mz + d) % NZ], zr.at[d], s_ss.at[2], s_rs.at[2], along_z(d)).start()
    zr[0] = tz[mz]
    reduce_start(2, 0)
    reduce_start(3, 0)

    plane_copy(lmid.at[others], lmid.at[others], s_ss.at[0], s_rs.at[0], me).wait_recv()
    for d in (4, 3, 5, 2, 6, 1, 7):
        plane_copy(lmid, lrecv.at[d], s_ss.at[3], s_rs.at[3], along_z(NZ - d)).start()
    lrecv[0] = lmid[...]

    reduce_wait(0)
    rs_s[4] = (g[1, 0] + rs_r[0].astype(f32)).astype(bf16)
    reduce_wait(1)
    rs_s[5] = (g[3, 1] + rs_r[1].astype(f32)).astype(bf16)

    plane_copy(zr.at[others], zr.at[others], s_ss.at[2], s_rs.at[2], me).wait_recv()
    xr[mx] = jnp.sum(zr[...], axis=0)
    for shift in (1, 2, 3):
        dp_copy(xr.at[mx], xr.at[mx], s_ss.at[4], s_rs.at[4], shift).start()

    reduce_start(2, 1)
    reduce_start(3, 1)

    three = pl.ds(0, NX - 1)
    dp_copy(xr.at[three], xr.at[three], s_ss.at[4], s_rs.at[4], 1).wait_recv()
    agz[mz] = (xr[0] + xr[1]) + (xr[2] + xr[3])
    for d in (4, 3, 5, 2, 6, 1, 7):
        plane_copy(agz.at[mz], agz.at[mz], s_ss.at[5], s_rs.at[5], along_z(d)).start()
    for n, h in ((4, 0), (5, 0), (4, 1), (5, 1)):
        reduce_start(n, h)

    plane_copy(lrecv.at[others], lrecv.at[others], s_ss.at[3], s_rs.at[3], me).wait_recv()
    table_f = jnp.concatenate(
        [lrecv[:, :, h].reshape(PLANE, HALF) for h in range(CHUNK // HALF)], axis=1
    )
    high = table_f.astype(bf16)
    left = table_f - high.astype(f32)
    middle = left.astype(bf16)
    low = (left - middle.astype(f32)).astype(bf16)
    spot = place[...] & (CHUNK - 1)
    turned = (qrow[...] & (NZ - 1)) * GROUP + (qrow[...] >> 3)
    hot = onehot(lax.broadcasted_iota(i32, (PLANE, ROWS), 0) == turned)
    seen = sum(
        lax.dot_general(part, hot, (((0,), (0,)), ((), ())), preferred_element_type=f32)
        for part in (high, middle, low)
    )
    loss_out[...] = jnp.sum(
        jnp.where(lax.broadcasted_iota(i32, (CHUNK, ROWS), 0) == spot, seen, 0.0),
        axis=0,
        keepdims=True,
    )

    plane_copy(agz.at[others], agz.at[others], s_ss.at[5], s_rs.at[5], me).wait_recv()
    for i in range(1, GROUP):
        plane_copy(agz, agb.at[mg], s_ss.at[6], s_rs.at[6], in_group(i)).start()
    agb[mg] = agz[...]

    reduce_wait(2)
    reduce_wait(3)
    reduce_wait(4)
    gout[0] = g[0, 0] + rs_r[3].astype(f32) + rs_r[4].astype(f32)
    reduce_wait(5)
    gout[1] = g[0, 1] + rs_r[2].astype(f32) + rs_r[5].astype(f32)

    plane_copy(agb.at[others], agb.at[others], s_ss.at[6], s_rs.at[6], me).wait_recv()
    for i in range(GROUP):
        for p in range(NZ):
            row, col = 32 * i + 8 * (p % 4), 128 * (p // 4)
            tg_out[row : row + 8, col : col + 128] = agb[i, p]

    for i in range(GROUP):
        for h in range(CHUNK // HALF):
            half(send, recv, i, h, i == 0 and h == 0).wait_send()
    for copy in gather + reduce:
        copy.wait_send()
    for n, ref in ((0, lmid), (1, tr), (2, zr), (3, lrecv), (5, agz), (6, agb)):
        plane_copy(ref.at[others], ref.at[others], s_ss.at[n], s_rs.at[n], me).wait_send()
    dp_copy(xr.at[three], xr.at[three], s_ss.at[4], s_rs.at[4], 1).wait_send()


def on_device(
    cell_table, sample_index, region, targets, trunk_weight, expert_params, first_moment, second_moment
):
    vmem = pl.BlockSpec(memory_space=pltpu.VMEM)
    hbm = pl.BlockSpec(memory_space=pltpu.HBM)
    dma = pltpu.SemaphoreType.DMA
    grads, losses, trunk_grad = pl.pallas_call(
        fused,
        out_shape=(
            jax.ShapeDtypeStruct((2, D, SHARE), f32),
            jax.ShapeDtypeStruct((1, ROWS), f32),
            jax.ShapeDtypeStruct((D, D), f32),
        ),
        in_specs=[hbm] * 6,
        out_specs=(vmem, vmem, vmem),
        scratch_shapes=[
            pltpu.VMEM((CELLS, D), bf16),
            pltpu.VMEM((2, D, SHARE), f32),
            pltpu.VMEM((1, ROWS), i32),
            pltpu.VMEM((1, ROWS), i32),
            pltpu.VMEM((D, D), bf16),
            dma((6,)),
            pltpu.VMEM((GROUP, CHUNK, 2 * D), bf16),
            pltpu.VMEM((GROUP, CHUNK, 2 * D), bf16),
            pltpu.VMEM((NX, 2, D, SHARE), bf16),
            pltpu.VMEM((NX, 2, SHARE, D), bf16),
            pltpu.VMEM((NX, 2, D, SHARE), f32),
            pltpu.VMEM((ROWS, 2 * D), bf16),
            pltpu.VMEM((1, ROWS), i32),
            pltpu.VMEM((1, ROWS), i32),
            pltpu.VMEM((NX, HALF, SHARE), bf16),
            pltpu.VMEM((NX, HALF, SHARE), f32),
            pltpu.VMEM((NX, HALF, SHARE), bf16),
            pltpu.VMEM((D, D), f32),
            pltpu.VMEM((6, D, SHARE), bf16),
            pltpu.VMEM((6, D, SHARE), bf16),
            pltpu.VMEM((GROUP, 32, D), f32),
            pltpu.VMEM((NZ, 8, 128), f32),
            pltpu.VMEM((NZ, 8, 128), f32),
            pltpu.VMEM((NX, 8, 128), f32),
            pltpu.VMEM((NZ, 8, 128), f32),
            pltpu.VMEM((GROUP, NZ, 8, 128), f32),
            pltpu.VMEM((GROUP, 1, 1, HALF), f32),
            pltpu.VMEM((GROUP, 1, 1, HALF), f32),
            pltpu.VMEM((NZ, GROUP, 1, 1, HALF), f32),
            dma((GROUP, 1)), dma((GROUP, 1)), pltpu.SemaphoreType.REGULAR,
            dma((6,)), dma((6,)),
            dma((6, 2)), dma((6, 2)),
            dma((7,)), dma((7,)),
        ],
        compiler_params=pltpu.CompilerParams(
            collective_id=0, has_side_effects=True, vmem_limit_bytes=36 << 20
        ),
        name="fused_step",
    )(
        *(
            pltpu.with_memory_space_constraint(value, pltpu.HBM)
            for value in (
                cell_table,
                sample_index.reshape(1, ROWS),
                region.reshape(1, ROWS),
                targets,
                trunk_weight,
                expert_params[0],
            )
        )
    )
    new_params, new_first, new_second = adam_update(
        expert_params, first_moment, second_moment, grads[None]
    )
    return (trunk_grad, losses.reshape(ROWS), new_params, new_first, new_second)


def solution(mesh):
    placed = (
        P(("dp", "expert"), None),
        P(("dp", "expert")),
        P(("dp", "expert"), None),
        P(("dp", "expert"), None),
        P(),
        P("expert", None, None, "dp"),
        P("expert", None, None, "dp"),
        P("expert", None, None, "dp"),
    )
    return jax.shard_map(
        on_device,
        mesh=mesh,
        in_specs=placed,
        out_specs=(
            P(),
            P(("dp", "expert")),
            P("expert", None, None, "dp"),
            P("expert", None, None, "dp"),
            P("expert", None, None, "dp"),
        ),
        check_vma=False,
    )
```
